128 devices in a mesh: pipe: 16 (over y, z_lo, core), fsdp: 8 (over z_hi, x).
Axes of the slice: x: 4, y: 4, z: 4 (z_hi: 2, z_lo: 2; z = z_hi * 2 + z_lo), core: 2. Of those that a mesh axis runs over, the one named last changes fastest.
Arguments:
- handoff_gradient: bfloat16 [16, 768, 8192], P('pipe', 'fsdp'), may hold values from -12 to 12
- output_weight: bfloat16 [16, 8192, 8192], P('pipe', 'fsdp'), may hold values from -0.0625 to 0.0625
- adapter_down: bfloat16 [16, 16, 8192], P('pipe', None, 'fsdp'), may hold values from -0.0625 to 0.0625
- adapter_up: bfloat16 [16, 16, 8192], P('pipe', None, 'fsdp'), may hold values from -0.29882812 to 0.29882812
- stored_queries: bfloat16 [16, 768, 8192], P('pipe', None, 'fsdp'), may hold values from -64 to 64
- stored_keys: bfloat16 [16, 768, 1024], P('pipe', None, 'fsdp'), may hold values from -3 to 3
- stored_values: bfloat16 [16, 768, 1024], P('pipe', None, 'fsdp'), may hold values from -6 to 6
- segments: int32 [16, 768], P('pipe'), may hold values from 0 to 7, never falling along the last dimension, each value on 1 to 384 neighbouring positions
Outputs:
- query_gradient: bfloat16 [16, 768, 8192], P('pipe', None, 'fsdp')
- key_gradient: bfloat16 [16, 768, 1024], P('pipe', None, 'fsdp')
- value_gradient: bfloat16 [16, 768, 1024], P('pipe', None, 'fsdp')
- down_map_gradient: float32 [16, 16, 8192], P('pipe', None, 'fsdp')
- up_map_gradient: float32 [16, 16, 8192], P('pipe', None, 'fsdp')
The draws below stay inside these ranges and needn't reach their ends.
Inputs may be any that keep to these rules, and one draw needn't show every extreme that they name: `segments`: ids never fall along a micro-batch.
All inputs are finite; a program needn't handle non-finite values.
Results may differ from the reference program's by a relative error of at most 0.015.
The reference program's roundings to bfloat16 on the way count: a program that leaves them out, or rounds other values in their place, can miss the bound.
Values may be sent and summed in bfloat16 or wider, within the bound.
A program may use at most 128 MiB of HBM per device.

```python
import math
import jax
import jax.numpy as jnp
import numpy as np
from jax import lax

MODEL_WIDTH = 8192
QUERY_HEADS = 64
VALUE_HEADS = 8
HEAD_SIZE = 128
ADAPTER_RANK = 16
DOCS = 8
MICRO_TOKENS = 768
N_PIPE = 16


def paired_draws(key):
    random_key_split = jax.random.fold_in(key, 101)
    key_queries = jax.random.fold_in(key, 202)
    random_key_draw = jnp.clip(jax.random.normal(random_key_split, (N_PIPE, MICRO_TOKENS, VALUE_HEADS, HEAD_SIZE), jnp.float32), -3.0, 3.0)
    query_rows = jnp.clip(jax.random.normal(key_queries, (N_PIPE, MICRO_TOKENS, QUERY_HEADS, HEAD_SIZE), jnp.float32), -4.0, 4.0)
    return (query_rows.reshape(N_PIPE, MICRO_TOKENS, QUERY_HEADS * HEAD_SIZE), random_key_draw.reshape(N_PIPE, MICRO_TOKENS, VALUE_HEADS * HEAD_SIZE))


def draw_stored_queries(key, part):
    return paired_draws(key)[0].astype(jnp.bfloat16)


def draw_stored_keys(key, part):
    return paired_draws(key)[1].astype(jnp.bfloat16)


def steps_of(own_key, extent, split, smallest, largest):
    def one(position, shards_of):
        draws = jax.random.uniform(jax.random.fold_in(jax.random.fold_in(own_key, 6), position), (shards_of,), jnp.float32, smallest / len(split), largest / len(split))
        return jnp.repeat(jnp.exp(draws), extent[position] // shards_of).reshape((-1,) + (1,) * (len(extent) - position - 1))

    gain = one(*split[0])
    for cut in split[1:]:
        gain = gain * one(*cut)
    return gain


def profile(amount, total, most, lean):
    weights = [(1 << 20) // math.isqrt(standing ** lean) + 1 for standing in range(2, amount + 1)]
    surplus, counts = total - most - (amount - 1), [1] * (amount - 1)
    while surplus > 0:
        free = [i for i in range(amount - 1) if counts[i] < most]
        pool, left = sum([weights[i] for i in free]), surplus
        for i in free:
            more = min(most - counts[i], max(1, left * weights[i] // pool), surplus)
            counts[i] = counts[i] + more
            surplus = surplus - more
    return np.array([most] + counts)


def ragged(key, amount, total, bound, skew):
    if amount == 2:
        one = jax.random.randint(key, (), max(1, total - bound), min(bound, total - 1) + 1)
        return jnp.stack([one, total - one])
    tallies = jnp.asarray(profile(amount, total, bound, skew), jnp.int32)
    couples = (amount - 1) // 2
    giver, sink = tallies[1:1 + 2 * couples:2], tallies[2:2 + 2 * couples:2]
    room = jnp.minimum(giver - 1, bound - sink)
    passed = jax.random.randint(jax.random.fold_in(key, 1), (couples,), 0, 1 << 20) % (room + 1)
    tallies = tallies.at[1:1 + 2 * couples:2].set(giver - passed).at[2:2 + 2 * couples:2].set(sink + passed)
    return tallies[jax.random.permutation(jax.random.fold_in(key, 2), amount)]


def bell_draw(own_key, extent, spread, most, shards=(), held_as=jnp.bfloat16):
    drawn = spread * jax.random.normal(own_key, extent, jnp.float32)
    if shards:
        drawn = drawn * steps_of(own_key, extent, shards, -0.22, 0.18)
    return jnp.clip(drawn, -most, most).astype(held_as)


def setup_inputs(seed: int = 0) -> dict:
    key_list = jax.random.split(jax.random.key(seed), 9)
    handoff_gradient = bell_draw(key_list[0], (N_PIPE, MICRO_TOKENS, MODEL_WIDTH), 2.0, 12.0, ((0, 16), (1, 8)))
    output_weight = bell_draw(key_list[1], (N_PIPE, QUERY_HEADS * HEAD_SIZE, MODEL_WIDTH), MODEL_WIDTH ** -0.5, 0.0625, ((0, 16), (1, 8)))
    adapter_down = bell_draw(key_list[2], (N_PIPE, ADAPTER_RANK, QUERY_HEADS * HEAD_SIZE), (QUERY_HEADS * HEAD_SIZE) ** -0.5, 0.0625, ((0, 16), (2, 8)))
    adapter_up = bell_draw(key_list[3], (N_PIPE, ADAPTER_RANK, MODEL_WIDTH), 0.05, 0.29882812, ((0, 16), (2, 8)))
    stored_queries = draw_stored_queries(jax.random.fold_in(key_list[8], 71), 0)
    stored_keys = draw_stored_keys(jax.random.fold_in(key_list[8], 71), 0)
    stored_values = bell_draw(key_list[6], (N_PIPE, MICRO_TOKENS, VALUE_HEADS * HEAD_SIZE), 1.0, 6.0, ((0, 16), (2, 8)))
    segments = jax.vmap(lambda own: jnp.searchsorted(jnp.cumsum(ragged(own, DOCS, MICRO_TOKENS, MICRO_TOKENS // 2, 1)), jnp.arange(MICRO_TOKENS), side="right"))(jax.random.split(key_list[7], N_PIPE)).reshape((N_PIPE, MICRO_TOKENS)).astype(jnp.int32)
    return {"handoff_gradient": handoff_gradient, "output_weight": output_weight, "adapter_down": adapter_down, "adapter_up": adapter_up, "stored_queries": stored_queries, "stored_keys": stored_keys, "stored_values": stored_values, "segments": segments}


adapter_scale = 2.0

def attend(query_block, key_head, value_head, context_gradient, allowed):
    inv_scale = 1.0 / math.sqrt(query_block.shape[-1])
    scores = jnp.einsum('bngd,snd->ngbs', query_block.astype(jnp.float32), key_head.astype(jnp.float32)) * inv_scale
    scores = jnp.where(allowed[None, None], scores, -jnp.inf)
    row_max = lax.optimization_barrier(jnp.max(scores, axis=-1, keepdims=True))
    expanded = jnp.exp(scores - row_max)
    attn_probs = expanded / lax.optimization_barrier(jnp.sum(expanded, axis=-1, keepdims=True))
    probs_low = lax.optimization_barrier(attn_probs.astype(jnp.bfloat16))
    context_rows = jnp.einsum('ngbs,snd->bngd', probs_low.astype(jnp.float32), value_head.astype(jnp.float32))
    context_rows = lax.optimization_barrier(context_rows.astype(jnp.bfloat16))
    grad_probs = jnp.einsum('bngd,snd->ngbs', context_gradient.astype(jnp.float32), value_head.astype(jnp.float32))
    row_delta = lax.optimization_barrier(jnp.sum(context_gradient.astype(jnp.float32) * context_rows.astype(jnp.float32), axis=-1))
    row_delta = jnp.transpose(row_delta, (1, 2, 0))[..., None]
    grad_scores = lax.optimization_barrier((attn_probs * (grad_probs - row_delta)).astype(jnp.bfloat16))
    grad_query = jnp.einsum('ngbs,snd->bngd', grad_scores.astype(jnp.float32), key_head.astype(jnp.float32))
    grad_query = (grad_query * inv_scale).astype(jnp.bfloat16)
    gradient_of_key = jnp.einsum('ngbs,bngd->snd', grad_scores.astype(jnp.float32), query_block.astype(jnp.float32)) * inv_scale
    gradient_of_value = jnp.einsum('ngbs,bngd->snd', probs_low.astype(jnp.float32), context_gradient.astype(jnp.float32))
    return (context_rows, grad_query, gradient_of_key, gradient_of_value)

def reference(handoff_gradient, output_weight, adapter_down, adapter_up, stored_queries, stored_keys, stored_values, segments):
    query_group_count = QUERY_HEADS // VALUE_HEADS
    positions = jnp.arange(MICRO_TOKENS)
    causal = positions[None, :] <= positions[:, None]
    result_list = ([], [], [], [], [])
    for section_number in range(N_PIPE):
        incoming_gradient = handoff_gradient[(section_number + 1) % N_PIPE]
        source_section = N_PIPE - 1 - section_number
        doc_ids = segments[section_number]
        allowed = causal & (doc_ids[:, None] == doc_ids[None, :])
        rank_gradient = jnp.dot(incoming_gradient, adapter_up[section_number].T, preferred_element_type=jnp.float32)
        frozen_portion = jnp.dot(incoming_gradient, output_weight[section_number].T, preferred_element_type=jnp.float32)
        rank_projected = jnp.dot(rank_gradient, adapter_down[section_number].astype(jnp.float32), precision=lax.Precision.HIGHEST)
        context_gradient = lax.optimization_barrier((frozen_portion + adapter_scale * rank_projected).astype(jnp.bfloat16))
        query_head_rows = stored_queries[source_section].reshape(MICRO_TOKENS, VALUE_HEADS, query_group_count, HEAD_SIZE).transpose(1, 0, 2, 3)[:, :, None]
        gradient_per_head = context_gradient.reshape(MICRO_TOKENS, VALUE_HEADS, query_group_count, HEAD_SIZE).transpose(1, 0, 2, 3)[:, :, None]
        key_head_rows = stored_keys[source_section].reshape(MICRO_TOKENS, VALUE_HEADS, HEAD_SIZE).transpose(1, 0, 2)[:, :, None]
        value_head_rows = stored_values[source_section].reshape(MICRO_TOKENS, VALUE_HEADS, HEAD_SIZE).transpose(1, 0, 2)[:, :, None]

        def one_head(head_items):
            return attend(head_items[0], head_items[1], head_items[2], head_items[3], allowed)
        context_rows, grad_query, gradient_of_key, gradient_of_value = lax.map(one_head, (query_head_rows, key_head_rows, value_head_rows, gradient_per_head))
        context_rows = context_rows.transpose(1, 0, 2, 3, 4).reshape(MICRO_TOKENS, QUERY_HEADS * HEAD_SIZE)
        grad_query = grad_query.transpose(1, 0, 2, 3, 4).reshape(MICRO_TOKENS, QUERY_HEADS * HEAD_SIZE)
        gradient_of_key = gradient_of_key.transpose(1, 0, 2, 3).reshape(MICRO_TOKENS, VALUE_HEADS * HEAD_SIZE).astype(jnp.bfloat16)
        gradient_of_value = gradient_of_value.transpose(1, 0, 2, 3).reshape(MICRO_TOKENS, VALUE_HEADS * HEAD_SIZE).astype(jnp.bfloat16)
        rank_context = jnp.dot(context_rows, adapter_down[section_number].T, preferred_element_type=jnp.float32)
        gradient_scale = adapter_scale / math.sqrt(MICRO_TOKENS)
        adapter_down_gradient = gradient_scale * jnp.dot(rank_gradient.T, context_rows.astype(jnp.float32), precision=lax.Precision.HIGHEST)
        adapter_up_gradient = gradient_scale * jnp.dot(rank_context.T, incoming_gradient.astype(jnp.float32), precision=lax.Precision.HIGHEST)
        result_list[0].append(grad_query)
        result_list[1].append(gradient_of_key)
        result_list[2].append(gradient_of_value)
        result_list[3].append(adapter_down_gradient)
        result_list[4].append(adapter_up_gradient)
    return (jnp.stack(result_list[0]), jnp.stack(result_list[1]), jnp.stack(result_list[2]), jnp.stack(result_list[3]), jnp.stack(result_list[4]))
```

```python
import functools
import math

import jax
import jax.numpy as jnp
from jax import lax
from jax.experimental import pallas as pl
from jax.experimental.pallas import tpu as pltpu
from jax.sharding import PartitionSpec as P

HEAD = 128
KEYS = 512
LORA_SCALE = 2.0
NEG = -1e30
LOG2E = math.log2(math.e)
F32 = jnp.float32
BF16 = jnp.bfloat16
HIGHEST = lax.Precision.HIGHEST
VMEM_BYTES = 44 << 20

NT = (((1,), (1,)), ((), ()))
TN = (((0,), (0,)), ((), ()))
NN = (((1,), (0,)), ((), ()))


def dot(a, b, dims, precision=None):
    return lax.dot_general(a, b, dims, precision=precision, preferred_element_type=F32)


def stack_heads(rows):
    heads = rows.shape[1] // HEAD
    return jnp.concatenate([rows[:, h * HEAD : (h + 1) * HEAD] for h in range(heads)], axis=0)


def unstack_heads(stacked, count):
    heads = stacked.shape[0] // count
    return jnp.concatenate([stacked[h * count : (h + 1) * count] for h in range(heads)], axis=1)


def window_start(block, rows):
    return pl.multiple_of(jnp.maximum(block * rows + rows - KEYS, 0), 32)


def allowed_keys(start, bounds):
    lanes = bounds.shape[1]
    position = start + lax.broadcasted_iota(jnp.int32, (KEYS, lanes), 0)
    return (position >= bounds[0:1]) & (position <= bounds[1:2])


def forward_kernel(rows, q_ref, k_ref, v_ref, bounds_ref, ctx_ref, lse_ref):
    start = window_start(pl.program_id(0), rows)
    keys = k_ref[pl.ds(start, KEYS), :]
    values = v_ref[pl.ds(start, KEYS), :]
    queries = stack_heads(q_ref[...])
    scores = dot(keys, queries, NT) * (LOG2E / math.sqrt(HEAD))
    scores = jnp.where(allowed_keys(start, bounds_ref[0]), scores, NEG)
    top = jnp.max(scores, axis=0, keepdims=True)
    expanded = jnp.exp2(scores - top)
    total = jnp.sum(expanded, axis=0, keepdims=True)
    probs = (expanded / total).astype(BF16)
    context = dot(values, probs, TN)
    ctx_ref[...] = unstack_heads(context.T.astype(BF16), rows)
    lse_ref[0] = top + jnp.log2(total)


def attention_forward(query, key, value, bounds):
    tokens, width = query.shape
    blocks, _, lanes = bounds.shape
    rows = tokens // blocks
    whole = pl.BlockSpec((tokens, HEAD), lambda i: (0, 0))
    return pl.pallas_call(
        functools.partial(forward_kernel, rows),
        grid=(blocks,),
        in_specs=[
            pl.BlockSpec((rows, width), lambda i: (i, 0)),
            whole,
            whole,
            pl.BlockSpec((1, 2, lanes), lambda i: (i, 0, 0)),
        ],
        out_specs=[
            pl.BlockSpec((rows, width), lambda i: (i, 0)),
            pl.BlockSpec((1, 1, lanes), lambda i: (i, 0, 0)),
        ],
        out_shape=[
            jax.ShapeDtypeStruct((tokens, width), BF16),
            jax.ShapeDtypeStruct((blocks, 1, lanes), F32),
        ],
        compiler_params=pltpu.CompilerParams(vmem_limit_bytes=VMEM_BYTES),
        cost_estimate=pl.CostEstimate(
            flops=4 * tokens * KEYS * width,
            bytes_accessed=4 * tokens * width,
            transcendentals=blocks * KEYS * lanes,
        ),
        name="attention_forward",
    )(query, key, value, bounds)


def project_kernel(parts, w_ref, up_ref, down_ref, *refs):
    x_refs = refs[:parts]
    g_ref, rank_ref, acc, rank_acc = refs[parts:]
    step = pl.program_id(0)
    x = jnp.concatenate([r[...] for r in x_refs], axis=0)
    product = dot(x, w_ref[...], NT)
    rank = dot(x, up_ref[...], NT)

    @pl.when(step == 0)
    def _():
        acc[...] = product
        rank_acc[...] = rank

    @pl.when(step > 0)
    def _():
        acc[...] += product
        rank_acc[...] += rank

    @pl.when(step == pl.num_programs(0) - 1)
    def _():
        projected = dot(rank_acc[...], down_ref[...].astype(F32), NN, HIGHEST)
        g_ref[...] = (acc[...] + LORA_SCALE * projected).astype(BF16)
        rank_ref[...] = rank_acc[...]


def project(xs, weight, up, down):
    features, depth = weight.shape
    ranks = up.shape[0]
    rows = sum(x.shape[0] for x in xs)
    chunk = 1024
    return pl.pallas_call(
        functools.partial(project_kernel, len(xs)),
        grid=(depth // chunk,),
        in_specs=[
            pl.BlockSpec((features, chunk), lambda i: (0, i)),
            pl.BlockSpec((ranks, chunk), lambda i: (0, i)),
            pl.BlockSpec((ranks, features), lambda i: (0, 0)),
        ]
        + [pl.BlockSpec((x.shape[0], chunk), lambda i: (0, i)) for x in xs],
        out_specs=[
            pl.BlockSpec((rows, features), lambda i: (0, 0)),
            pl.BlockSpec((rows, ranks), lambda i: (0, 0)),
        ],
        out_shape=[
            jax.ShapeDtypeStruct((rows, features), BF16),
            jax.ShapeDtypeStruct((rows, ranks), F32),
        ],
        scratch_shapes=[pltpu.VMEM((rows, features), F32), pltpu.VMEM((rows, ranks), F32)],
        compiler_params=pltpu.CompilerParams(vmem_limit_bytes=VMEM_BYTES),
        cost_estimate=pl.CostEstimate(
            flops=2 * rows * features * depth,
            bytes_accessed=2 * features * depth + 2 * rows * depth,
            transcendentals=0,
        ),
        name="project",
    )(weight, up, down, *xs)


def backward_kernel(first, last, rows, where_ref, *refs):
    q_ref, ctx_ref, lse_ref, bounds_ref, g_ref, rank_ref, k_ref, v_ref = refs[:8]
    refs = refs[8:]
    if not first:
        dq_in, dk_in, dv_in, dm_in = refs[:4]
        refs = refs[4:]
    dq_ref, dk_ref, dv_ref, dm_ref, dk, dv, dm = refs
    step = pl.program_id(0)

    @pl.when(step == 0)
    def _():
        if first:
            dk[...] = jnp.zeros_like(dk)
            dv[...] = jnp.zeros_like(dv)
            dm[...] = jnp.zeros_like(dm)
        else:
            dk[...] = dk_in[...]
            dv[...] = dv_in[...]
            dm[...] = dm_in[...]

    start = window_start(where_ref[step], rows)
    window = pl.ds(start, KEYS)
    keys = k_ref[window, :]
    values = v_ref[window, :]
    queries = stack_heads(q_ref[...])
    gradient = stack_heads(g_ref[...])
    context = stack_heads(ctx_ref[...])
    products = gradient.astype(F32) * context.astype(F32)
    delta = dot(jnp.ones((8, HEAD), F32), products, NT, HIGHEST)[0:1]
    scores = dot(keys, queries, NT) * (LOG2E / math.sqrt(HEAD))
    shifted = jnp.where(allowed_keys(start, bounds_ref[0]), scores - lse_ref[0], NEG)
    probs = jnp.exp2(shifted)
    grad_probs = dot(values, gradient, NT)
    grad_scores = (probs * (grad_probs - delta)).astype(BF16)
    dv[window, :] += dot(probs.astype(BF16), gradient, NN)
    dk[window, :] += dot(grad_scores, queries, NN)
    grad_query = dot(keys, grad_scores, TN) * (1.0 / math.sqrt(HEAD))
    dq_ref[...] = unstack_heads(grad_query.T.astype(BF16), rows)
    dm[...] += dot(rank_ref[...], ctx_ref[...].astype(F32), TN, HIGHEST)

    @pl.when(step == pl.num_programs(0) - 1)
    def _():
        if last:
            tokens = k_ref.shape[0]
            dk_ref[...] = (dk[...] * (1.0 / math.sqrt(HEAD))).astype(BF16)
            dv_ref[...] = dv[...].astype(BF16)
            dm_ref[...] = dm[...] * (LORA_SCALE / math.sqrt(tokens))
        else:
            dk_ref[...] = dk[...]
            dv_ref[...] = dv[...]
            dm_ref[...] = dm[...]


def attention_backward(where, query, context, lse, bounds, gradient, rank, key, value, carried, last):
    tokens, width = query.shape
    blocks, _, lanes = bounds.shape
    rows = tokens // blocks
    ranks = rank.shape[1]
    steps = gradient.shape[0] // rows
    first = carried is None
    whole = pl.BlockSpec((tokens, HEAD), lambda i, w: (0, 0))
    small = pl.BlockSpec((ranks, width), lambda i, w: (0, 0))
    picked = pl.BlockSpec((rows, width), lambda i, w: (w[i], 0))
    in_specs = [
        picked,
        picked,
        pl.BlockSpec((1, 1, lanes), lambda i, w: (w[i], 0, 0)),
        pl.BlockSpec((1, 2, lanes), lambda i, w: (w[i], 0, 0)),
        pl.BlockSpec((rows, width), lambda i, w: (i, 0)),
        pl.BlockSpec((rows, ranks), lambda i, w: (i, 0)),
        whole,
        whole,
    ]
    operands = [query, context, lse, bounds, gradient, rank, key, value]
    aliases = {}
    if not first:
        in_specs += [pl.BlockSpec(memory_space=pl.ANY), whole, whole, small]
        operands += list(carried)
        aliases = {9: 0}
    kv_type = BF16 if last else F32
    return pl.pallas_call(
        functools.partial(backward_kernel, first, last, rows),
        grid_spec=pltpu.PrefetchScalarGridSpec(
            num_scalar_prefetch=1,
            grid=(steps,),
            in_specs=in_specs,
            out_specs=[picked, whole, whole, small],
            scratch_shapes=[
                pltpu.VMEM((tokens, HEAD), F32),
                pltpu.VMEM((tokens, HEAD), F32),
                pltpu.VMEM((ranks, width), F32),
            ],
        ),
        out_shape=[
            jax.ShapeDtypeStruct((tokens, width), BF16),
            jax.ShapeDtypeStruct((tokens, HEAD), kv_type),
            jax.ShapeDtypeStruct((tokens, HEAD), kv_type),
            jax.ShapeDtypeStruct((ranks, width), F32),
        ],
        input_output_aliases=aliases,
        compiler_params=pltpu.CompilerParams(vmem_limit_bytes=VMEM_BYTES),
        cost_estimate=pl.CostEstimate(
            flops=10 * steps * rows * KEYS * width,
            bytes_accessed=10 * steps * rows * width,
            transcendentals=steps * KEYS * lanes,
        ),
        name="attention_backward",
    )(where, *operands)


def up_map_kernel(where_ref, member_ref, *refs):
    rank_ref, x_ref, out_ref = refs[0], refs[1:-1], refs[-1]
    rows = rank_ref.shape[0] // 8
    total = None
    offset = 0
    for ref in x_ref:
        count = ref.shape[0]
        block, inner = offset // rows, offset % rows
        begin = pl.multiple_of(where_ref[block] * rows + inner, 16)
        part = dot(rank_ref[pl.ds(begin, count), :], ref[...].astype(F32), TN, HIGHEST)
        total = part if total is None else total + part
        offset += count
    out_ref[...] = total * (LORA_SCALE / math.sqrt(rank_ref.shape[0]))


def up_map(where, member, rank_context, xs, width):
    tokens, ranks = rank_context.shape
    return pl.pallas_call(
        up_map_kernel,
        grid_spec=pltpu.PrefetchScalarGridSpec(
            num_scalar_prefetch=2,
            grid=(1,),
            in_specs=[pl.BlockSpec((tokens, ranks), lambda i, w, m: (0, 0))]
            + [pl.BlockSpec((x.shape[0], width), lambda i, w, m: (0, m[0])) for x in xs],
            out_specs=pl.BlockSpec((ranks, width), lambda i, w, m: (0, 0)),
        ),
        out_shape=jax.ShapeDtypeStruct((ranks, width), F32),
        compiler_params=pltpu.CompilerParams(vmem_limit_bytes=VMEM_BYTES),
        name="up_map",
    )(where, member, rank_context, *xs)


def per_device(
    handoff_gradient,
    output_weight,
    adapter_down,
    adapter_up,
    stored_queries,
    stored_keys,
    stored_values,
    segments,
):
    stages = lax.axis_size("pipe")
    members = lax.axis_size("fsdp")
    ring = members // 2
    both = ("pipe", "fsdp")
    member = lax.axis_index("fsdp")
    shard = handoff_gradient[0]
    rows = shard.shape[0]
    half = rows // 2
    tokens = rows * members
    heads = stored_queries.shape[2] // HEAD

    def from_next(block, flip):
        route = []
        for p in range(stages):
            for f in range(members):
                source = ((p + 1) % stages) * members + (f + flip) % members
                route.append((source, p * members + f))
        return lax.ppermute(block, both, route)

    def along_x(block, distance):
        route = []
        for f in range(members):
            plane, x = divmod(f, ring)
            route.append((plane * ring + (x - distance) % ring, f))
        return lax.ppermute(block, "fsdp", route)

    def mirrored(block):
        return lax.ppermute(block, "pipe", [(i, stages - 1 - i) for i in range(stages)])

    near = from_next(shard, 0)
    across = from_next(shard, ring)
    query = mirrored(stored_queries[0])
    key = mirrored(stored_keys[0])
    value = mirrored(stored_values[0])
    up_whole = lax.all_gather(adapter_up[0], "fsdp", axis=1, tiled=True)
    down = adapter_down[0]

    left0 = along_x(near, 1)
    right0 = along_x(near, -1)
    left1 = along_x(across, 1)
    right1 = along_x(across, -1)
    far0 = (along_x(left0[:half], 1), along_x(right0[half:], -1))
    far1 = (along_x(left1[:half], 1), along_x(right1[half:], -1))

    plane, x = member // ring, member % ring

    def pair(shift):
        column = (x + shift) % ring
        return jnp.stack([plane * ring + column, (1 - plane) * ring + column]).astype(jnp.int32)

    doc = segments[0]
    position = jnp.arange(tokens, dtype=jnp.int32)
    begin = jnp.sum((doc[None, :] < doc[:, None]).astype(jnp.int32), axis=1)
    bounds = jnp.stack([begin, position]).reshape(2, members, rows)
    bounds = jnp.tile(bounds.transpose(1, 0, 2), (1, 1, heads))

    weight = output_weight[0]
    context, lse = attention_forward(query, key, value, bounds)
    rank_context = lax.dot_general(down, context, NT, preferred_element_type=F32)
    for partner in (1, 2, ring):
        route = [(f, f ^ partner) for f in range(members)]
        rank_context = rank_context + lax.ppermute(rank_context, "fsdp", route)

    groups = [
        (pair(0), [near, across]),
        (pair(-1), [left0, left1]),
        (pair(1), [right0, right1]),
        (pair(2), [far0[0], far0[1], far1[0], far1[1]]),
    ]
    carried = None
    for number, (where, xs) in enumerate(groups):
        gradient, rank = project(xs, weight, up_whole, down)
        carried = attention_backward(
            where,
            query,
            context,
            lse,
            bounds,
            gradient,
            rank,
            key,
            value,
            carried,
            number == len(groups) - 1,
        )
    query_gradient, key_gradient, value_gradient, down_map_gradient = carried
    up_map_gradient = up_map(
        jnp.concatenate([where for where, _ in groups]),
        member.reshape(1).astype(jnp.int32),
        rank_context.T,
        [x for _, xs in groups for x in xs],
        adapter_up.shape[2],
    )
    return (
        query_gradient[None],
        key_gradient[None],
        value_gradient[None],
        down_map_gradient[None],
        up_map_gradient[None],
    )


def solution(mesh):
    split = P("pipe", None, "fsdp")
    rows = P("pipe", "fsdp", None)
    return jax.shard_map(
        per_device,
        mesh=mesh,
        in_specs=(rows, rows, split, split, split, split, split, P("pipe", None)),
        out_specs=(split,) * 5,
        check_vma=False,
    )
```

```python
import functools
import math

import jax
import jax.numpy as jnp
from jax import lax
from jax.experimental import pallas as pl
from jax.experimental.pallas import tpu as pltpu
from jax.sharding import PartitionSpec as P

HEAD = 128
KEYS = 512
LORA_SCALE = 2.0
NEG = -1e30
LOG2E = math.log2(math.e)
F32 = jnp.float32
BF16 = jnp.bfloat16
HIGHEST = lax.Precision.HIGHEST
VMEM_BYTES = 60 << 20

NT = (((1,), (1,)), ((), ()))
TN = (((0,), (0,)), ((), ()))
NN = (((1,), (0,)), ((), ()))


def dot(a, b, dims, precision=None):
    return lax.dot_general(a, b, dims, precision=precision, preferred_element_type=F32)


def stack_heads(rows):
    heads = rows.shape[1] // HEAD
    return jnp.concatenate([rows[:, h * HEAD : (h + 1) * HEAD] for h in range(heads)], axis=0)


def unstack_heads(stacked, count):
    heads = stacked.shape[0] // count
    return jnp.concatenate([stacked[h * count : (h + 1) * count] for h in range(heads)], axis=1)


def window_start(block, rows):
    return pl.multiple_of(jnp.maximum(block * rows + rows - KEYS, 0), 32)


def allowed_keys(start, bounds):
    lanes = bounds.shape[1]
    position = start + lax.broadcasted_iota(jnp.int32, (KEYS, lanes), 0)
    return (position >= bounds[0:1]) & (position <= bounds[1:2])


def forward_kernel(rows, q_ref, k_ref, v_ref, bounds_ref, down_ref, ctx_ref, lse_ref, rank_ref, rank):
    step = pl.program_id(0)
    start = window_start(step, rows)
    keys = k_ref[pl.ds(start, KEYS), :]
    values = v_ref[pl.ds(start, KEYS), :]
    queries = stack_heads(q_ref[...])
    scores = dot(keys, queries, NT) * (LOG2E / math.sqrt(HEAD))
    scores = jnp.where(allowed_keys(start, bounds_ref[0]), scores, NEG)
    top = jnp.max(scores, axis=0, keepdims=True)
    expanded = jnp.exp2(scores - top)
    total = jnp.sum(expanded, axis=0, keepdims=True)
    probs = (expanded / total).astype(BF16)
    context = dot(values, probs, TN)
    context = unstack_heads(context.T.astype(BF16), rows)
    ctx_ref[...] = context
    lse_ref[0] = top + jnp.log2(total)
    rank[pl.ds(pl.multiple_of(step * rows, 32), rows), :] = dot(context, down_ref[...], NT)

    @pl.when(step == pl.num_programs(0) - 1)
    def _():
        rank_ref[...] = rank[...].T


def attention_forward(query, key, value, bounds, down):
    tokens, width = query.shape
    ranks = down.shape[0]
    blocks, _, lanes = bounds.shape
    rows = tokens // blocks
    whole = pl.BlockSpec((tokens, HEAD), lambda i: (0, 0))
    return pl.pallas_call(
        functools.partial(forward_kernel, rows),
        grid=(blocks,),
        in_specs=[
            pl.BlockSpec((rows, width), lambda i: (i, 0)),
            whole,
            whole,
            pl.BlockSpec((1, 2, lanes), lambda i: (i, 0, 0)),
            pl.BlockSpec((ranks, width), lambda i: (0, 0)),
        ],
        out_specs=[
            pl.BlockSpec((rows, width), lambda i: (i, 0)),
            pl.BlockSpec((1, 1, lanes), lambda i: (i, 0, 0)),
            pl.BlockSpec((ranks, tokens), lambda i: (0, 0)),
        ],
        out_shape=[
            jax.ShapeDtypeStruct((tokens, width), BF16),
            jax.ShapeDtypeStruct((blocks, 1, lanes), F32),
            jax.ShapeDtypeStruct((ranks, tokens), F32),
        ],
        scratch_shapes=[pltpu.VMEM((tokens, ranks), F32)],
        compiler_params=pltpu.CompilerParams(vmem_limit_bytes=VMEM_BYTES),
        name="attention_forward",
    )(query, key, value, bounds, down)


def project_kernel(last, parts, where_ref, member_ref, w_ref, up_ref, down_ref, *refs):
    x_refs = refs[:parts]
    refs = refs[parts:]
    if last:
        context_ref, partial_ref, g_ref, rank_ref, map_ref, acc, rank_acc = refs
    else:
        g_ref, rank_ref, acc, rank_acc = refs
    step = pl.program_id(0)
    x = jnp.concatenate([r[...] for r in x_refs], axis=0)
    product = dot(w_ref[...], x, NT)
    rank = dot(up_ref[0], x, NT)

    @pl.when(step == 0)
    def _():
        acc[...] = product
        rank_acc[...] = rank

    @pl.when(step > 0)
    def _():
        acc[...] += product
        rank_acc[...] += rank

    if last:

        @pl.when(step == member_ref[0])
        def _():
            total = up_map_terms(where_ref, context_ref, x_refs)
            map_ref[...] = (partial_ref[...] + total) * (LORA_SCALE / math.sqrt(context_ref.shape[0]))

    @pl.when(step == pl.num_programs(0) - 1)
    def _():
        projected = dot(down_ref[...].astype(F32), rank_acc[...], TN, HIGHEST)
        g_ref[...] = (acc[...] + LORA_SCALE * projected).T.astype(BF16)
        rank_ref[...] = rank_acc[...].T


def up_map_terms(where_ref, context_ref, x_refs):
    total = None
    for index, ref in enumerate(x_refs):
        count = ref.shape[0]
        begin = pl.multiple_of(where_ref[index] * count, 32)
        part = dot(context_ref[pl.ds(begin, count), :], ref[...].astype(F32), TN, HIGHEST)
        total = part if total is None else total + part
    return total


def project(where, member, xs, weight, up, down, up_map_parts=None):
    features, depth = weight.shape
    members, ranks, chunk = up.shape
    rows = sum(x.shape[0] for x in xs)
    last = up_map_parts is not None
    extra = list(up_map_parts) if last else []
    whole = [pl.BlockSpec(e.shape, lambda i, w, m: (0, 0)) for e in extra]
    out_specs = [
        pl.BlockSpec((rows, features), lambda i, w, m: (0, 0)),
        pl.BlockSpec((rows, ranks), lambda i, w, m: (0, 0)),
    ]
    out_shape = [
        jax.ShapeDtypeStruct((rows, features), BF16),
        jax.ShapeDtypeStruct((rows, ranks), F32),
    ]
    if last:
        out_specs.append(pl.BlockSpec((ranks, chunk), lambda i, w, m: (0, 0)))
        out_shape.append(jax.ShapeDtypeStruct((ranks, chunk), F32))
    return pl.pallas_call(
        functools.partial(project_kernel, last, len(xs)),
        grid_spec=pltpu.PrefetchScalarGridSpec(
            num_scalar_prefetch=2,
            grid=(members,),
            in_specs=[
                pl.BlockSpec((features, chunk), lambda i, w, m: (0, i)),
                pl.BlockSpec((1, ranks, chunk), lambda i, w, m: (i, 0, 0)),
                pl.BlockSpec((ranks, features), lambda i, w, m: (0, 0)),
            ]
            + [pl.BlockSpec((x.shape[0], chunk), lambda i, w, m: (0, i)) for x in xs]
            + whole,
            out_specs=out_specs,
            scratch_shapes=[pltpu.VMEM((features, rows), F32), pltpu.VMEM((ranks, rows), F32)],
        ),
        out_shape=out_shape,
        compiler_params=pltpu.CompilerParams(vmem_limit_bytes=VMEM_BYTES),
        name="project",
    )(where, member, weight, up, down, *xs, *extra)


def backward_kernel(first, last, rows, where_ref, *refs):
    q_ref, ctx_ref, lse_ref, bounds_ref, g_ref, rank_ref, k_ref, v_ref = refs[:8]
    refs = refs[8:]
    if not first:
        dq_in, dk_in, dv_in, dm_in = refs[:4]
        refs = refs[4:]
    dq_ref, dk_ref, dv_ref, dm_ref, dk, dv, dm = refs
    step = pl.program_id(0)

    @pl.when(step == 0)
    def _():
        if first:
            dk[...] = jnp.zeros_like(dk)
            dv[...] = jnp.zeros_like(dv)
            dm[...] = jnp.zeros_like(dm)
        else:
            dk[...] = dk_in[...]
            dv[...] = dv_in[...]
            dm[...] = dm_in[...]

    start = window_start(where_ref[step], rows)
    window = pl.ds(start, KEYS)
    keys = k_ref[window, :]
    values = v_ref[window, :]
    queries = stack_heads(q_ref[...])
    gradient = stack_heads(g_ref[...])
    context = stack_heads(ctx_ref[...])
    products = gradient.astype(F32) * context.astype(F32)
    delta = dot(jnp.ones((8, HEAD), F32), products, NT, HIGHEST)[0:1]
    scores = dot(keys, queries, NT) * (LOG2E / math.sqrt(HEAD))
    shifted = jnp.where(allowed_keys(start, bounds_ref[0]), scores - lse_ref[0], NEG)
    probs = jnp.exp2(shifted)
    grad_probs = dot(values, gradient, NT)
    grad_scores = (probs * (grad_probs - delta)).astype(BF16)
    dv[window, :] += dot(probs.astype(BF16), gradient, NN)
    dk[window, :] += dot(grad_scores, queries, NN)
    grad_query = dot(keys, grad_scores, TN) * (1.0 / math.sqrt(HEAD))
    dq_ref[...] = unstack_heads(grad_query.T.astype(BF16), rows)
    dm[...] += dot(rank_ref[...], ctx_ref[...].astype(F32), TN, HIGHEST)

    @pl.when(step == pl.num_programs(0) - 1)
    def _():
        if last:
            tokens = k_ref.shape[0]
            dk_ref[...] = (dk[...] * (1.0 / math.sqrt(HEAD))).astype(BF16)
            dv_ref[...] = dv[...].astype(BF16)
            dm_ref[...] = dm[...] * (LORA_SCALE / math.sqrt(tokens))
        else:
            dk_ref[...] = dk[...]
            dv_ref[...] = dv[...]
            dm_ref[...] = dm[...]


def attention_backward(where, query, context, lse, bounds, gradient, rank, key, value, carried, last):
    tokens, width = query.shape
    blocks, _, lanes = bounds.shape
    rows = tokens // blocks
    ranks = rank.shape[1]
    steps = gradient.shape[0] // rows
    first = carried is None
    whole = pl.BlockSpec((tokens, HEAD), lambda i, w: (0, 0))
    small = pl.BlockSpec((ranks, width), lambda i, w: (0, 0))
    picked = pl.BlockSpec((rows, width), lambda i, w: (w[i], 0))
    in_specs = [
        picked,
        picked,
        pl.BlockSpec((1, 1, lanes), lambda i, w: (w[i], 0, 0)),
        pl.BlockSpec((1, 2, lanes), lambda i, w: (w[i], 0, 0)),
        pl.BlockSpec((rows, width), lambda i, w: (i, 0)),
        pl.BlockSpec((rows, ranks), lambda i, w: (i, 0)),
        whole,
        whole,
    ]
    operands = [query, context, lse, bounds, gradient, rank, key, value]
    aliases = {}
    if not first:
        in_specs += [pl.BlockSpec(memory_space=pl.ANY), whole, whole, small]
        operands += list(carried)
        aliases = {9: 0}
    kv_type = BF16 if last else F32
    return pl.pallas_call(
        functools.partial(backward_kernel, first, last, rows),
        grid_spec=pltpu.PrefetchScalarGridSpec(
            num_scalar_prefetch=1,
            grid=(steps,),
            in_specs=in_specs,
            out_specs=[picked, whole, whole, small],
            scratch_shapes=[
                pltpu.VMEM((tokens, HEAD), F32),
                pltpu.VMEM((tokens, HEAD), F32),
                pltpu.VMEM((ranks, width), F32),
            ],
        ),
        out_shape=[
            jax.ShapeDtypeStruct((tokens, width), BF16),
            jax.ShapeDtypeStruct((tokens, HEAD), kv_type),
            jax.ShapeDtypeStruct((tokens, HEAD), kv_type),
            jax.ShapeDtypeStruct((ranks, width), F32),
        ],
        input_output_aliases=aliases,
        compiler_params=pltpu.CompilerParams(vmem_limit_bytes=VMEM_BYTES),
        name="attention_backward",
    )(where, *operands)


def up_map_kernel(where_ref, member_ref, gathered_ref, *refs):
    x_refs, context_ref, out_ref = refs[:-2], refs[-2], refs[-1]
    context_ref[...] = gathered_ref[...].T
    out_ref[...] = up_map_terms(where_ref, context_ref, x_refs)


def up_map(where, member, gathered, xs, width):
    ranks, tokens = gathered.shape
    return pl.pallas_call(
        up_map_kernel,
        grid_spec=pltpu.PrefetchScalarGridSpec(
            num_scalar_prefetch=2,
            grid=(1,),
            in_specs=[pl.BlockSpec((ranks, tokens), lambda i, w, m: (0, 0))]
            + [pl.BlockSpec((x.shape[0], width), lambda i, w, m: (0, m[0])) for x in xs],
            out_specs=[
                pl.BlockSpec((tokens, ranks), lambda i, w, m: (0, 0)),
                pl.BlockSpec((ranks, width), lambda i, w, m: (0, 0)),
            ],
        ),
        out_shape=[
            jax.ShapeDtypeStruct((tokens, ranks), F32),
            jax.ShapeDtypeStruct((ranks, width), F32),
        ],
        compiler_params=pltpu.CompilerParams(vmem_limit_bytes=VMEM_BYTES),
        name="up_map",
    )(where, member, gathered, *xs)


def per_device(
    handoff_gradient,
    output_weight,
    adapter_down,
    adapter_up,
    stored_queries,
    stored_keys,
    stored_values,
    segments,
):
    stages = lax.axis_size("pipe")
    members = lax.axis_size("fsdp")
    ring = members // 2
    both = ("pipe", "fsdp")
    member = lax.axis_index("fsdp")
    shard = handoff_gradient[0]
    rows = shard.shape[0]
    tokens = rows * members
    heads = stored_queries.shape[2] // HEAD

    def from_next(block, flip):
        route = []
        for p in range(stages):
            for f in range(members):
                source = ((p + 1) % stages) * members + (f + flip) % members
                route.append((source, p * members + f))
        return lax.ppermute(block, both, route)

    def along_x(block, distance):
        route = []
        for f in range(members):
            plane, x = divmod(f, ring)
            route.append((plane * ring + (x - distance) % ring, f))
        return lax.ppermute(block, "fsdp", route)

    def mirrored(block):
        return lax.ppermute(block, "pipe", [(i, stages - 1 - i) for i in range(stages)])

    def after(values, others):
        return lax.optimization_barrier((tuple(values), tuple(others)))[0]

    def exchanged(block, partner):
        return lax.ppermute(block, "fsdp", [(f, f ^ partner) for f in range(members)])

    def gather_small(block):
        for bit, partner in enumerate((1, 2, ring)):
            other = exchanged(block, partner)
            low = (member >> bit) % 2 == 0
            block = jnp.where(
                low, jnp.concatenate([block, other]), jnp.concatenate([other, block])
            )
        return block

    up_whole = gather_small(adapter_up)

    down = adapter_down[0]
    weight = output_weight[0]

    near = from_next(shard, 0)
    left0 = along_x(near, 1)
    right0 = along_x(near, -1)
    second, parked_query, parked_key, parked_value = after(
        (shard, stored_queries[0], stored_keys[0], stored_values[0]), (near,)
    )
    across = from_next(second, ring)
    query = mirrored(parked_query)
    key = mirrored(parked_key)
    value = mirrored(parked_value)
    far0 = along_x(left0, 1)
    (across_later,) = after((across,), (left0, right0))
    left1 = along_x(across_later, 1)
    right1 = along_x(across_later, -1)
    far1 = along_x(right1, -1)

    plane, x = member // ring, member % ring

    def pair(shift):
        column = (x + shift) % ring
        return jnp.stack([plane * ring + column, (1 - plane) * ring + column]).astype(jnp.int32)

    doc = segments[0]
    position = jnp.arange(tokens, dtype=jnp.int32)
    begin = jnp.sum((doc[None, :] < doc[:, None]).astype(jnp.int32), axis=1)
    bounds = jnp.stack([begin, position]).reshape(2, members, rows)
    bounds = jnp.tile(bounds.transpose(1, 0, 2), (1, 1, heads))
    me = member.reshape(1).astype(jnp.int32)

    groups = [
        (pair(0), [near, across]),
        (pair(-1), [left0, left1]),
        (pair(1), [right0, right1]),
    ]
    projected = [project(where, me, xs, weight, up_whole, down) for where, xs in groups]
    query, key, value = after((query, key, value), [g for g, _ in projected])
    context, lse, rank_part = attention_forward(query, key, value, bounds, down)
    for partner in (1, 2, ring):
        rank_part = rank_part + exchanged(rank_part, partner)
    carried = None
    for (where, _), (gradient, rank) in zip(groups, projected):
        carried = attention_backward(
            where, query, context, lse, bounds, gradient, rank, key, value, carried, False
        )
    rank_context, partial = up_map(
        jnp.concatenate([where for where, _ in groups]),
        me,
        rank_part,
        [x for _, xs in groups for x in xs],
        adapter_up.shape[2],
    )
    where = pair(2)
    far0, far1 = after((far0, far1), (carried[3], partial))
    gradient, rank, up_map_gradient = project(
        where, me, [far0, far1], weight, up_whole, down, (rank_context, partial)
    )
    query_gradient, key_gradient, value_gradient, down_map_gradient = attention_backward(
        where, query, context, lse, bounds, gradient, rank, key, value, carried, True
    )
    return (
        query_gradient[None],
        key_gradient[None],
        value_gradient[None],
        down_map_gradient[None],
        up_map_gradient[None],
    )


def solution(mesh):
    split = P("pipe", None, "fsdp")
    rows = P("pipe", "fsdp", None)
    return jax.shard_map(
        per_device,
        mesh=mesh,
        in_specs=(rows, rows, split, split, split, split, split, P("pipe", None)),
        out_specs=(split,) * 5,
        check_vma=False,
    )
```

```python
import functools
import math

import jax
import jax.numpy as jnp
from jax import lax
from jax.experimental import pallas as pl
from jax.experimental.pallas import tpu as pltpu
from jax.sharding import PartitionSpec as P

HEAD = 128
KEYS = 512
CHUNKS = 4
LORA_SCALE = 2.0
NEG = -1e30
LOG2E = math.log2(math.e)
F32 = jnp.float32
BF16 = jnp.bfloat16
HIGHEST = lax.Precision.HIGHEST
MESH = pl.DeviceIdType.MESH
VMEM_BYTES = 60 << 20

NT = (((1,), (1,)), ((), ()))
TN = (((0,), (0,)), ((), ()))
NN = (((1,), (0,)), ((), ()))

NEAR, ACROSS, RIGHT0, RIGHT1, FAR0, FAR1, LEFT0, LEFT1 = range(8)


def dot(a, b, dims, precision=None):
    return lax.dot_general(a, b, dims, precision=precision, preferred_element_type=F32)


def stack_heads(rows):
    heads = rows.shape[1] // HEAD
    return jnp.concatenate([rows[:, h * HEAD : (h + 1) * HEAD] for h in range(heads)], axis=0)


def unstack_heads(stacked, count):
    heads = stacked.shape[0] // count
    return jnp.concatenate([stacked[h * count : (h + 1) * count] for h in range(heads)], axis=1)


def kernel(
    stages,
    members,
    shard,
    weight_hbm,
    down,
    up_hbm,
    query_hbm,
    key_hbm,
    value_hbm,
    segments,
    dq_ref,
    dk_ref,
    dv_ref,
    down_map_ref,
    up_map_ref,
    x_ref,
    weight,
    up,
    query,
    key,
    value,
    doc,
    context,
    lse,
    gradient,
    rank,
    acc,
    rank_acc,
    dq,
    dk,
    dv,
    rank_context,
    rank_sum,
    rank_parts,
    shard_send,
    shard_recv,
    parked_send,
    parked_recv,
    up_send,
    up_recv,
    rank_send,
    rank_recv,
    weight_sem,
    up_sem,
    dq_sem,
):
    pipe = lax.axis_index("pipe")
    member = lax.axis_index("fsdp")
    ring = members // 2
    plane, x = member // ring, member % ring
    rows, depth = shard.shape
    tokens, width = query_hbm.shape
    heads = width // HEAD
    ranks = down.shape[0]
    lanes = heads * rows
    wide = depth // CHUNKS
    local = depth // members
    before = (pipe + stages - 1) % stages
    behind = (pipe + 1) % stages
    flipped = (member + ring) % members
    to_left = plane * ring + (x + ring - 1) % ring
    to_right = plane * ring + (x + 1) % ring

    def device(p, f):
        return {"pipe": p, "fsdp": f}

    barrier = pltpu.get_barrier_semaphore()
    partners = [
        (before, member),
        (before, flipped),
        (behind, member),
        (behind, flipped),
        (stages - 1 - pipe, member),
    ]
    partners += [(pipe, (member + i) % members) for i in range(1, members)]
    for p, f in partners:
        pl.semaphore_signal(barrier, inc=1, device_id=device(p, f), device_id_type=MESH)

    def weight_copy(i):
        part = pl.ds(pl.multiple_of(i * local, local), local)
        return pltpu.make_async_copy(
            weight_hbm.at[:, part], weight.at[:, part], weight_sem.at[i]
        )

    @pl.loop(0, members)
    def _(i):
        weight_copy(i).start()

    own_up = pltpu.make_async_copy(up_hbm, up.at[member], up_sem)
    own_up.start()

    routes = {
        NEAR: (shard, before, member),
        ACROSS: (shard, before, flipped),
        RIGHT0: (x_ref.at[NEAR], pipe, to_left),
        LEFT0: (x_ref.at[NEAR], pipe, to_right),
        RIGHT1: (x_ref.at[ACROSS], pipe, to_left),
        LEFT1: (x_ref.at[ACROSS], pipe, to_right),
        FAR0: (x_ref.at[LEFT0], pipe, to_right),
        FAR1: (x_ref.at[RIGHT1], pipe, to_left),
    }

    def columns(c):
        return pl.ds(pl.multiple_of(c * wide, wide), wide)

    def hop(slot, c):
        source, p, f = routes[slot]
        return pltpu.make_async_remote_copy(
            src_ref=source.at[:, columns(c)],
            dst_ref=x_ref.at[slot, :, columns(c)],
            send_sem=shard_send.at[slot, c],
            recv_sem=shard_recv.at[slot, c],
            device_id=device(p, f),
            device_id_type=MESH,
        )

    def up_copy(i):
        return pltpu.make_async_remote_copy(
            src_ref=up_hbm,
            dst_ref=up.at[member],
            send_sem=up_send.at[i - 1],
            recv_sem=up_recv.at[i - 1],
            device_id=device(pipe, (member + i) % members),
            device_id_type=MESH,
        )

    parked = [
        pltpu.make_async_remote_copy(
            src_ref=source,
            dst_ref=target,
            send_sem=parked_send.at[i],
            recv_sem=parked_recv.at[i],
            device_id=device(stages - 1 - pipe, member),
            device_id_type=MESH,
        )
        for i, (source, target) in enumerate(
            [(key_hbm, key), (value_hbm, value), (query_hbm, query)]
        )
    ]

    def rank_copy(i):
        peer = flipped if i == 0 else plane * ring + (x + i) % ring
        return pltpu.make_async_remote_copy(
            src_ref=rank_sum.at[1 if i == 0 else 0],
            dst_ref=rank_parts.at[i],
            send_sem=rank_send.at[i],
            recv_sem=rank_recv.at[i],
            device_id=device(pipe, peer),
            device_id_type=MESH,
        )

    pl.semaphore_wait(barrier, len(partners))

    @pl.loop(0, CHUNKS)
    def _(c):
        hop(NEAR, c).start()

    for i in range(1, members):
        up_copy(i).start()

    ids = jnp.broadcast_to(segments[...].astype(F32), (8, tokens))
    doc[...] = ids.T

    @pl.loop(0, CHUNKS)
    def _(c):
        hop(NEAR, c).wait_recv()
        hop(RIGHT0, c).start()
        hop(LEFT0, c).start()

    @pl.loop(0, CHUNKS)
    def _(c):
        hop(ACROSS, c).start()

    def relay(c):
        hop(LEFT0, c).wait_recv()
        hop(FAR0, c).start()
        hop(ACROSS, c).wait_recv()
        hop(RIGHT1, c).start()
        hop(LEFT1, c).start()

    relay(0)
    for copy in parked:
        copy.start()
    pl.loop(1, CHUNKS)(relay)

    def block_of(slot):
        side = (plane + slot) % 2
        return side * ring + (x + slot // 2) % ring

    def project_chunk(group, c):
        rows_in = jnp.concatenate(
            [x_ref[2 * group, :, columns(c)], x_ref[2 * group + 1, :, columns(c)]], axis=0
        )
        up_rows = [up[members // CHUNKS * c + i] for i in range(members // CHUNKS)]
        acc[...] += dot(weight[:, columns(c)], rows_in, NT)
        rank_acc[...] += dot(jnp.concatenate(up_rows, axis=1), rows_in, NT)

    def project_start():
        acc[...] = jnp.zeros_like(acc)
        rank_acc[...] = jnp.zeros_like(rank_acc)

    def project_end(group):
        projected = dot(down[...].astype(F32), rank_acc[...], TN, HIGHEST)
        total = (acc[...] + LORA_SCALE * projected).T.astype(BF16)
        ranked = rank_acc[...].T
        for i in range(2):
            gradient[2 * group + i] = total[i * rows : (i + 1) * rows]
            rank[2 * group + i] = ranked[i * rows : (i + 1) * rows]

    def project(group):
        project_start()
        pl.loop(0, CHUNKS)(functools.partial(project_chunk, group))
        project_end(group)

    own_up.wait()
    for i in range(1, members):
        up_copy(i).wait_recv()

    @pl.loop(0, members)
    def _(i):
        weight_copy(i).wait()

    project(NEAR // 2)

    @pl.loop(0, CHUNKS)
    def _(c):
        hop(RIGHT1, c).wait_recv()
        hop(FAR1, c).start()

    def arrived(slot):
        @pl.loop(0, CHUNKS)
        def _(c):
            hop(slot, c).wait_recv()

    arrived(RIGHT0)
    project(RIGHT0 // 2)
    arrived(LEFT1)
    project(LEFT0 // 2)

    def token_rows(block):
        return pl.ds(pl.multiple_of(block * rows, 32), rows)

    def key_window(block):
        begin = (block // (KEYS // rows)) * (block * rows + rows - KEYS)
        return pl.multiple_of(begin, 32)

    def allowed_keys(block, begin):
        lane = lax.broadcasted_iota(jnp.int32, (rows, lanes), 1) % rows
        spread = (lax.broadcasted_iota(jnp.int32, (rows, lanes), 0) == lane).astype(F32)
        own = dot(doc[token_rows(block), :], spread, TN)[0:1]
        other = doc[pl.ds(begin, KEYS), 0:1]
        place = block * rows + lane[0:1]
        position = begin + lax.broadcasted_iota(jnp.int32, (KEYS, lanes), 0)
        return (position <= place) & (other == own)

    def scores_of(block, begin):
        queries = stack_heads(query[token_rows(block), :])
        scores = dot(key[pl.ds(begin, KEYS), :], queries, NT) * (LOG2E / math.sqrt(HEAD))
        return queries, scores

    for copy in parked:
        copy.wait_recv()

    @pl.loop(0, members)
    def _(block):
        begin = key_window(block)
        _, scores = scores_of(block, begin)
        scores = jnp.where(allowed_keys(block, begin), scores, NEG)
        top = jnp.max(scores, axis=0, keepdims=True)
        expanded = jnp.exp2(scores - top)
        total = jnp.sum(expanded, axis=0, keepdims=True)
        probs = (expanded / total).astype(BF16)
        mixed = dot(value[pl.ds(begin, KEYS), :], probs, TN)
        mixed = unstack_heads(mixed.T.astype(BF16), rows)
        context[token_rows(block), :] = mixed
        lse[block] = top + jnp.log2(total)
        rank_context[token_rows(block), :] = dot(mixed, down[...], NT)

    rank_sum[0] = rank_context[...].T
    for i in range(1, ring):
        rank_copy(i).start()

    dk[...] = jnp.zeros_like(dk)
    dv[...] = jnp.zeros_like(dv)
    down_map_ref[...] = jnp.zeros_like(down_map_ref)
    up_map_ref[...] = jnp.zeros_like(up_map_ref)

    def dq_copy(slot):
        block = block_of(slot)
        return pltpu.make_async_copy(
            dq.at[token_rows(block), :], dq_ref.at[token_rows(block), :], dq_sem.at[slot]
        )

    def backward(slot):
        block = block_of(slot)
        begin = key_window(block)
        window = pl.ds(begin, KEYS)
        queries, scores = scores_of(block, begin)
        arriving = stack_heads(gradient[slot])
        mixed = context[token_rows(block), :]
        products = arriving.astype(F32) * stack_heads(mixed).astype(F32)
        delta = dot(jnp.ones((8, HEAD), F32), products, NT, HIGHEST)[0:1]
        shifted = jnp.where(allowed_keys(block, begin), scores - lse[block], NEG)
        probs = jnp.exp2(shifted)
        grad_probs = dot(value[window, :], arriving, NT)
        grad_scores = (probs * (grad_probs - delta)).astype(BF16)
        dv[window, :] += dot(probs.astype(BF16), arriving, NN)
        dk[window, :] += dot(grad_scores, queries, NN)
        grad_query = dot(key[window, :], grad_scores, TN) * (1.0 / math.sqrt(HEAD))
        dq[token_rows(block), :] = unstack_heads(grad_query.T.astype(BF16), rows)
        down_map_ref[...] += dot(rank[slot], mixed.astype(F32), TN, HIGHEST)
        dq_copy(slot).start()

    def up_map(slot):
        part = x_ref[slot, :, pl.ds(pl.multiple_of(member * local, local), local)]
        ranked = rank_context[token_rows(block_of(slot)), :]
        up_map_ref[...] += dot(ranked, part.astype(F32), TN, HIGHEST)

    pl.loop(NEAR, ACROSS + 1)(backward)
    for i in range(1, ring):
        rank_copy(i).wait_recv()
    rank_sum[1] = rank_sum[0] + rank_parts[1] + rank_parts[2] + rank_parts[3]
    rank_copy(0).start()
    pl.loop(RIGHT0, RIGHT1 + 1)(backward)
    pl.loop(LEFT0, LEFT1 + 1)(backward)
    rank_copy(0).wait_recv()
    rank_context[...] = (rank_sum[1] + rank_parts[0]).T
    pl.loop(NEAR, RIGHT1 + 1)(up_map)
    pl.loop(LEFT0, LEFT1 + 1)(up_map)

    project_start()

    @pl.loop(0, CHUNKS)
    def _(c):
        hop(FAR0, c).wait_recv()
        hop(FAR1, c).wait_recv()
        project_chunk(FAR0 // 2, c)

    project_end(FAR0 // 2)
    pl.loop(FAR0, FAR1 + 1)(backward)
    pl.loop(FAR0, FAR1 + 1)(up_map)

    dk_ref[...] = (dk[...] * (1.0 / math.sqrt(HEAD))).astype(BF16)
    dv_ref[...] = dv[...].astype(BF16)
    scale = LORA_SCALE / math.sqrt(tokens)
    down_map_ref[...] = down_map_ref[...] * scale
    up_map_ref[...] = up_map_ref[...] * scale

    for slot in range(members):

        @pl.loop(0, CHUNKS)
        def _(c):
            hop(slot, c).wait_send()

        dq_copy(slot).wait()
    for copy in parked:
        copy.wait_send()
    for i in range(1, members):
        up_copy(i).wait_send()
    for i in range(ring):
        rank_copy(i).wait_send()


def per_device(
    handoff_gradient,
    output_weight,
    adapter_down,
    adapter_up,
    stored_queries,
    stored_keys,
    stored_values,
    segments,
):
    stages = lax.axis_size("pipe")
    members = lax.axis_size("fsdp")
    rows, depth = handoff_gradient.shape[1:]
    tokens, width = stored_queries.shape[1:]
    ranks = adapter_down.shape[1]
    local = adapter_up.shape[2]
    lanes = width // HEAD * rows
    anywhere = pl.BlockSpec(memory_space=pl.ANY)
    on_chip = pl.BlockSpec(memory_space=pltpu.VMEM)
    dma = pltpu.SemaphoreType.DMA
    outputs = pl.pallas_call(
        functools.partial(kernel, stages, members),
        in_specs=[anywhere, anywhere, on_chip, anywhere, anywhere, anywhere, anywhere, on_chip],
        out_specs=[anywhere, on_chip, on_chip, on_chip, on_chip],
        out_shape=[
            jax.ShapeDtypeStruct((tokens, width), BF16),
            jax.ShapeDtypeStruct((tokens, HEAD), BF16),
            jax.ShapeDtypeStruct((tokens, HEAD), BF16),
            jax.ShapeDtypeStruct((ranks, width), F32),
            jax.ShapeDtypeStruct((ranks, local), F32),
        ],
        scratch_shapes=[
            pltpu.VMEM((members, rows, depth), BF16),
            pltpu.VMEM((width, depth), BF16),
            pltpu.VMEM((members, ranks, local), BF16),
            pltpu.VMEM((tokens, width), BF16),
            pltpu.VMEM((tokens, HEAD), BF16),
            pltpu.VMEM((tokens, HEAD), BF16),
            pltpu.VMEM((tokens, 8), F32),
            pltpu.VMEM((tokens, width), BF16),
            pltpu.VMEM((members, 1, lanes), F32),
            pltpu.VMEM((members, rows, width), BF16),
            pltpu.VMEM((members, rows, ranks), F32),
            pltpu.VMEM((width, 2 * rows), F32),
            pltpu.VMEM((ranks, 2 * rows), F32),
            pltpu.VMEM((tokens, width), BF16),
            pltpu.VMEM((tokens, HEAD), F32),
            pltpu.VMEM((tokens, HEAD), F32),
            pltpu.VMEM((tokens, ranks), F32),
            pltpu.VMEM((2, ranks, tokens), F32),
            pltpu.VMEM((4, ranks, tokens), F32),
            dma((members, CHUNKS)),
            dma((members, CHUNKS)),
            dma((3,)),
            dma((3,)),
            dma((members - 1,)),
            dma((members - 1,)),
            dma((4,)),
            dma((4,)),
            dma((members,)),
            dma,
            dma((members,)),
        ],
        compiler_params=pltpu.CompilerParams(
            collective_id=0, has_side_effects=True, vmem_limit_bytes=VMEM_BYTES
        ),
        name="relay",
    )(
        handoff_gradient[0],
        output_weight[0],
        adapter_down[0],
        adapter_up[0],
        stored_queries[0],
        stored_keys[0],
        stored_values[0],
        segments,
    )
    return tuple(output[None] for output in outputs)


def solution(mesh):
    split = P("pipe", None, "fsdp")
    rows = P("pipe", "fsdp", None)
    return jax.shard_map(
        per_device,
        mesh=mesh,
        in_specs=(rows, rows, split, split, split, split, split, P("pipe", None)),
        out_specs=(split,) * 5,
        check_vma=False,
    )
```

```python
import functools
import math

import jax
import jax.numpy as jnp
from jax import lax
from jax.experimental import pallas as pl
from jax.experimental.pallas import tpu as pltpu
from jax.sharding import PartitionSpec as P

HEAD = 128
KEYS = 512
CHUNKS = 4
LORA_SCALE = 2.0
NEG = -1e30
LOG2E = math.log2(math.e)
F32 = jnp.float32
BF16 = jnp.bfloat16
HIGHEST = lax.Precision.HIGHEST
MESH = pl.DeviceIdType.MESH
VMEM_BYTES = 60 << 20

NT = (((1,), (1,)), ((), ()))
TN = (((0,), (0,)), ((), ()))
NN = (((1,), (0,)), ((), ()))

NEAR, ACROSS, RIGHT0, RIGHT1, FAR0, FAR1, LEFT0, LEFT1 = range(8)


def dot(a, b, dims, precision=None):
    return lax.dot_general(a, b, dims, precision=precision, preferred_element_type=F32)


def stack_heads(rows):
    heads = rows.shape[1] // HEAD
    return jnp.concatenate([rows[:, h * HEAD : (h + 1) * HEAD] for h in range(heads)], axis=0)


def unstack_heads(stacked, count):
    heads = stacked.shape[0] // count
    return jnp.concatenate([stacked[h * count : (h + 1) * count] for h in range(heads)], axis=1)


def kernel(
    stages,
    members,
    shard,
    weight_hbm,
    down,
    up_hbm,
    query_hbm,
    key_hbm,
    value_hbm,
    segments,
    dq_ref,
    dk_ref,
    dv_ref,
    down_map_ref,
    up_map_ref,
    x_ref,
    weight,
    up,
    query,
    key,
    value,
    doc,
    context,
    lse,
    gradient,
    rank,
    acc,
    rank_acc,
    dq,
    dk,
    dv,
    rank_context,
    rank_sum,
    rank_parts,
    shard_send,
    shard_recv,
    parked_send,
    parked_recv,
    up_send,
    up_recv,
    rank_send,
    rank_recv,
    weight_sem,
    up_sem,
    dq_sem,
):
    pipe = lax.axis_index("pipe")
    member = lax.axis_index("fsdp")
    ring = members // 2
    plane, x = member // ring, member % ring
    rows, depth = shard.shape
    tokens, width = query_hbm.shape
    heads = width // HEAD
    ranks = down.shape[0]
    lanes = heads * rows
    wide = depth // CHUNKS
    local = depth // members
    before = (pipe + stages - 1) % stages
    behind = (pipe + 1) % stages
    flipped = (member + ring) % members
    to_left = plane * ring + (x + ring - 1) % ring
    to_right = plane * ring + (x + 1) % ring

    def device(p, f):
        return {"pipe": p, "fsdp": f}

    barrier = pltpu.get_barrier_semaphore()
    partners = [
        (before, member),
        (before, flipped),
        (behind, member),
        (behind, flipped),
        (stages - 1 - pipe, member),
    ]
    partners += [(pipe, (member + i) % members) for i in range(1, members)]
    for p, f in partners:
        pl.semaphore_signal(barrier, inc=1, device_id=device(p, f), device_id_type=MESH)

    def weight_copy(i):
        part = pl.ds(pl.multiple_of(i * local, local), local)
        return pltpu.make_async_copy(
            weight_hbm.at[:, part], weight.at[:, part], weight_sem.at[i]
        )

    @pl.loop(0, members)
    def _(i):
        weight_copy(i).start()

    own_up = pltpu.make_async_copy(up_hbm, up.at[member], up_sem)
    own_up.start()

    routes = {
        NEAR: (shard, before, member),
        ACROSS: (shard, before, flipped),
        RIGHT0: (x_ref.at[NEAR], pipe, to_left),
        LEFT0: (x_ref.at[NEAR], pipe, to_right),
        RIGHT1: (x_ref.at[ACROSS], pipe, to_left),
        LEFT1: (x_ref.at[ACROSS], pipe, to_right),
        FAR0: (x_ref.at[LEFT0], pipe, to_right),
        FAR1: (x_ref.at[LEFT1], pipe, to_right),
    }
    mirrored = {
        FAR0: (x_ref.at[RIGHT0], pipe, to_left),
        FAR1: (x_ref.at[RIGHT1], pipe, to_left),
    }

    def columns(c):
        return pl.ds(pl.multiple_of(c * wide, wide), wide)

    def hop(slot, c, table=routes):
        source, p, f = table[slot]
        return pltpu.make_async_remote_copy(
            src_ref=source.at[:, columns(c)],
            dst_ref=x_ref.at[slot, :, columns(c)],
            send_sem=shard_send.at[slot, c],
            recv_sem=shard_recv.at[slot, c],
            device_id=device(p, f),
            device_id_type=MESH,
        )

    def up_copy(i):
        return pltpu.make_async_remote_copy(
            src_ref=up_hbm,
            dst_ref=up.at[member],
            send_sem=up_send.at[i - 1],
            recv_sem=up_recv.at[i - 1],
            device_id=device(pipe, (member + i) % members),
            device_id_type=MESH,
        )

    parked = [
        pltpu.make_async_remote_copy(
            src_ref=source,
            dst_ref=target,
            send_sem=parked_send.at[i],
            recv_sem=parked_recv.at[i],
            device_id=device(stages - 1 - pipe, member),
            device_id_type=MESH,
        )
        for i, (source, target) in enumerate(
            [(key_hbm, key), (value_hbm, value), (query_hbm, query)]
        )
    ]

    def rank_copy(i):
        peer = flipped if i == 0 else plane * ring + (x + i) % ring
        return pltpu.make_async_remote_copy(
            src_ref=rank_sum.at[1 if i == 0 else 0],
            dst_ref=rank_parts.at[i],
            send_sem=rank_send.at[i],
            recv_sem=rank_recv.at[i],
            device_id=device(pipe, peer),
            device_id_type=MESH,
        )

    pl.semaphore_wait(barrier, len(partners))

    even = pipe % 2 == 0

    @pl.loop(0, CHUNKS)
    def _(c):
        hop(NEAR, c).start()

    def send_across():
        @pl.loop(0, CHUNKS)
        def _(c):
            hop(ACROSS, c).start()

    pl.when(even)(send_across)
    for i in range(1, members):
        up_copy(i).start()

    ids = jnp.broadcast_to(segments[...].astype(F32), (8, tokens))
    doc[...] = ids.T

    @pl.loop(0, CHUNKS)
    def _(c):
        hop(NEAR, c).wait_recv()
        hop(RIGHT0, c).start()
        hop(LEFT0, c).start()

    def relay_across():
        @pl.loop(0, CHUNKS)
        def _(c):
            hop(ACROSS, c).wait_recv()
            hop(RIGHT1, c).start()
            hop(LEFT1, c).start()

    def relay_far(far, left, right, c):
        hop(left, c).wait_recv()
        hop(far, c).start()
        hop(right, c + 1).wait_recv()
        hop(far, c + 1, mirrored).start()

    def send_parked():
        for copy in parked:
            copy.start()

    def relay_far_all(far, left, right):
        @pl.loop(0, CHUNKS, step=2)
        def _(c):
            relay_far(far, left, right, c)

    odd = pipe % 2 == 1

    @pl.when(even)
    def _():
        relay_far_all(FAR0, LEFT0, RIGHT0)
        send_parked()

    @pl.when(odd)
    def _():
        send_across()
        send_parked()
        relay_across()
        relay_far_all(FAR0, LEFT0, RIGHT0)

    def block_of(slot):
        side = (plane + slot) % 2
        return side * ring + (x + slot // 2) % ring

    def project_chunk(slots, c):
        used = pl.ds(0, len(slots) * rows)
        rows_in = jnp.concatenate([x_ref[slot, :, columns(c)] for slot in slots], axis=0)
        up_rows = [up[members // CHUNKS * c + i] for i in range(members // CHUNKS)]
        product = dot(weight[:, columns(c)], rows_in, NT)
        ranked = dot(jnp.concatenate(up_rows, axis=1), rows_in, NT)
        acc[:, used] = acc[:, used] + product
        rank_acc[:, used] = rank_acc[:, used] + ranked

    def project_start():
        acc[...] = jnp.zeros_like(acc)
        rank_acc[...] = jnp.zeros_like(rank_acc)

    def project_end(slots):
        used = pl.ds(0, len(slots) * rows)
        projected = dot(down[...].astype(F32), rank_acc[:, used], TN, HIGHEST)
        total = (acc[:, used] + LORA_SCALE * projected).T.astype(BF16)
        ranked = rank_acc[:, used].T
        for i, slot in enumerate(slots):
            gradient[slot] = total[i * rows : (i + 1) * rows]
            rank[slot] = ranked[i * rows : (i + 1) * rows]

    own_up.wait()
    for i in range(1, members):
        up_copy(i).wait_recv()

    @pl.loop(0, members)
    def _(i):
        weight_copy(i).wait()

    own = (NEAR, RIGHT0, FAR0, LEFT0)
    project_start()

    @pl.loop(0, CHUNKS, step=2)
    def _(c):
        hop(RIGHT0, c).wait_recv()
        hop(FAR0, c).wait_recv()
        project_chunk(own, c)
        hop(LEFT0, c + 1).wait_recv()
        hop(FAR0, c + 1).wait_recv()
        project_chunk(own, c + 1)

    project_end(own)

    @pl.when(even)
    def _():
        relay_across()

    @pl.when(odd)
    def _():
        relay_far_all(FAR1, LEFT1, RIGHT1)

    def token_rows(block):
        return pl.ds(pl.multiple_of(block * rows, 32), rows)

    def key_window(block):
        begin = (block // (KEYS // rows)) * (block * rows + rows - KEYS)
        return pl.multiple_of(begin, 32)

    def allowed_keys(block, begin, reach=KEYS):
        lane = lax.broadcasted_iota(jnp.int32, (rows, lanes), 1) % rows
        spread = (lax.broadcasted_iota(jnp.int32, (rows, lanes), 0) == lane).astype(F32)
        own = dot(doc[token_rows(block), :], spread, TN)[0:1]
        other = doc[pl.ds(begin, reach), 0:1]
        place = block * rows + lane[0:1]
        position = begin + lax.broadcasted_iota(jnp.int32, (reach, lanes), 0)
        return (position <= place) & (other == own)

    def scores_of(block, begin, reach=KEYS):
        queries = stack_heads(query[token_rows(block), :])
        scores = dot(key[pl.ds(begin, reach), :], queries, NT) * (LOG2E / math.sqrt(HEAD))
        return queries, scores

    for copy in parked:
        copy.wait_recv()

    def forward(reach, block):
        begin = key_window(block)
        _, scores = scores_of(block, begin, reach)
        scores = jnp.where(allowed_keys(block, begin, reach), scores, NEG)
        top = jnp.max(scores, axis=0, keepdims=True)
        expanded = jnp.exp2(scores - top)
        total = jnp.sum(expanded, axis=0, keepdims=True)
        probs = (expanded / total).astype(BF16)
        mixed = dot(value[pl.ds(begin, reach), :], probs, TN)
        mixed = unstack_heads(mixed.T.astype(BF16), rows)
        context[token_rows(block), :] = mixed
        lse[block] = top + jnp.log2(total)
        rank_context[token_rows(block), :] = dot(mixed, down[...], NT)

    done = 0
    for reach in (KEYS // 2, 3 * KEYS // 4, KEYS):
        until = members if reach == KEYS else reach // rows
        pl.loop(done, until)(functools.partial(forward, reach))
        done = until

    rank_sum[0] = rank_context[...].T
    for i in range(1, ring):
        rank_copy(i).start()

    dk[...] = jnp.zeros_like(dk)
    dv[...] = jnp.zeros_like(dv)
    down_map_ref[...] = jnp.zeros_like(down_map_ref)
    up_map_ref[...] = jnp.zeros_like(up_map_ref)

    def dq_copy(slot):
        block = block_of(slot)
        return pltpu.make_async_copy(
            dq.at[token_rows(block), :], dq_ref.at[token_rows(block), :], dq_sem.at[slot]
        )

    def backward(slot):
        block = block_of(slot)
        begin = key_window(block)
        window = pl.ds(begin, KEYS)
        queries, scores = scores_of(block, begin)
        arriving = stack_heads(gradient[slot])
        mixed = context[token_rows(block), :]
        products = arriving.astype(F32) * stack_heads(mixed).astype(F32)
        delta = dot(jnp.ones((8, HEAD), F32), products, NT, HIGHEST)[0:1]
        shifted = jnp.where(allowed_keys(block, begin), scores - lse[block], NEG)
        probs = jnp.exp2(shifted)
        grad_probs = dot(value[window, :], arriving, NT)
        grad_scores = (probs * (grad_probs - delta)).astype(BF16)
        dv[window, :] += dot(probs.astype(BF16), arriving, NN)
        dk[window, :] += dot(grad_scores, queries, NN)
        grad_query = dot(key[window, :], grad_scores, TN) * (1.0 / math.sqrt(HEAD))
        dq[token_rows(block), :] = unstack_heads(grad_query.T.astype(BF16), rows)
        down_map_ref[...] += dot(rank[slot], mixed.astype(F32), TN, HIGHEST)
        dq_copy(slot).start()

    def up_map(slot):
        part = x_ref[slot, :, pl.ds(pl.multiple_of(member * local, local), local)]
        ranked = rank_context[token_rows(block_of(slot)), :]
        up_map_ref[...] += dot(ranked, part.astype(F32), TN, HIGHEST)

    @pl.when(even)
    def _():
        relay_far_all(FAR1, LEFT1, RIGHT1)

    pl.loop(NEAR, FAR0, step=2)(backward)
    for i in range(1, ring):
        rank_copy(i).wait_recv()
    rank_sum[1] = rank_sum[0] + rank_parts[1] + rank_parts[2] + rank_parts[3]
    rank_copy(0).start()
    pl.loop(FAR0, members, step=2)(backward)
    project_start()

    @pl.loop(0, CHUNKS, step=2)
    def _(c):
        hop(RIGHT1, c).wait_recv()
        project_chunk((ACROSS, RIGHT1), c)
        project_chunk((ACROSS, RIGHT1), c + 1)

    project_end((ACROSS, RIGHT1))
    pl.loop(ACROSS, FAR1, step=2)(backward)
    rank_copy(0).wait_recv()
    rank_context[...] = (rank_sum[1] + rank_parts[0]).T
    pl.loop(NEAR, FAR1)(up_map)
    up_map(LEFT0)
    project_start()

    @pl.loop(0, CHUNKS, step=2)
    def _(c):
        hop(FAR1, c).wait_recv()
        project_chunk((FAR1, LEFT1), c)
        hop(LEFT1, c + 1).wait_recv()
        hop(FAR1, c + 1).wait_recv()
        project_chunk((FAR1, LEFT1), c + 1)

    project_end((FAR1, LEFT1))
    pl.loop(FAR1, members, step=2)(backward)
    pl.loop(FAR1, members, step=2)(up_map)

    dk_ref[...] = (dk[...] * (1.0 / math.sqrt(HEAD))).astype(BF16)
    dv_ref[...] = dv[...].astype(BF16)
    scale = LORA_SCALE / math.sqrt(tokens)
    down_map_ref[...] = down_map_ref[...] * scale
    up_map_ref[...] = up_map_ref[...] * scale

    for slot in range(members):

        @pl.loop(0, CHUNKS)
        def _(c):
            hop(slot, c).wait_send()

        dq_copy(slot).wait()
    for copy in parked:
        copy.wait_send()
    for i in range(1, members):
        up_copy(i).wait_send()
    for i in range(ring):
        rank_copy(i).wait_send()


def per_device(
    handoff_gradient,
    output_weight,
    adapter_down,
    adapter_up,
    stored_queries,
    stored_keys,
    stored_values,
    segments,
):
    stages = lax.axis_size("pipe")
    members = lax.axis_size("fsdp")
    rows, depth = handoff_gradient.shape[1:]
    tokens, width = stored_queries.shape[1:]
    ranks = adapter_down.shape[1]
    local = adapter_up.shape[2]
    lanes = width // HEAD * rows
    anywhere = pl.BlockSpec(memory_space=pl.ANY)
    on_chip = pl.BlockSpec(memory_space=pltpu.VMEM)
    dma = pltpu.SemaphoreType.DMA
    outputs = pl.pallas_call(
        functools.partial(kernel, stages, members),
        in_specs=[anywhere, anywhere, on_chip, anywhere, anywhere, anywhere, anywhere, on_chip],
        out_specs=[anywhere, on_chip, on_chip, on_chip, on_chip],
        out_shape=[
            jax.ShapeDtypeStruct((tokens, width), BF16),
            jax.ShapeDtypeStruct((tokens, HEAD), BF16),
            jax.ShapeDtypeStruct((tokens, HEAD), BF16),
            jax.ShapeDtypeStruct((ranks, width), F32),
            jax.ShapeDtypeStruct((ranks, local), F32),
        ],
        scratch_shapes=[
            pltpu.VMEM((members, rows, depth), BF16),
            pltpu.VMEM((width, depth), BF16),
            pltpu.VMEM((members, ranks, local), BF16),
            pltpu.VMEM((tokens, width), BF16),
            pltpu.VMEM((tokens, HEAD), BF16),
            pltpu.VMEM((tokens, HEAD), BF16),
            pltpu.VMEM((tokens, 8), F32),
            pltpu.VMEM((tokens, width), BF16),
            pltpu.VMEM((members, 1, lanes), F32),
            pltpu.VMEM((members, rows, width), BF16),
            pltpu.VMEM((members, rows, ranks), F32),
            pltpu.VMEM((width, 4 * rows), F32),
            pltpu.VMEM((ranks, 4 * rows), F32),
            pltpu.VMEM((tokens, width), BF16),
            pltpu.VMEM((tokens, HEAD), F32),
            pltpu.VMEM((tokens, HEAD), F32),
            pltpu.VMEM((tokens, ranks), F32),
            pltpu.VMEM((2, ranks, tokens), F32),
            pltpu.VMEM((4, ranks, tokens), F32),
            dma((members, CHUNKS)),
            dma((members, CHUNKS)),
            dma((3,)),
            dma((3,)),
            dma((members - 1,)),
            dma((members - 1,)),
            dma((4,)),
            dma((4,)),
            dma((members,)),
            dma,
            dma((members,)),
        ],
        compiler_params=pltpu.CompilerParams(
            collective_id=0, has_side_effects=True, vmem_limit_bytes=VMEM_BYTES
        ),
        name="relay",
    )(
        handoff_gradient[0],
        output_weight[0],
        adapter_down[0],
        adapter_up[0],
        stored_queries[0],
        stored_keys[0],
        stored_values[0],
        segments,
    )
    return tuple(output[None] for output in outputs)


def solution(mesh):
    split = P("pipe", None, "fsdp")
    rows = P("pipe", "fsdp", None)
    return jax.shard_map(
        per_device,
        mesh=mesh,
        in_specs=(rows, rows, split, split, split, split, split, P("pipe", None)),
        out_specs=(split,) * 5,
        check_vma=False,
    )
```

```python
import functools
import math

import jax
import jax.numpy as jnp
from jax import lax
from jax.experimental import pallas as pl
from jax.experimental.pallas import tpu as pltpu
from jax.sharding import PartitionSpec as P

HEAD = 128
KEYS = 512
CHUNKS = 4
LORA_SCALE = 2.0
NEG = -1e30
LOG2E = math.log2(math.e)
F32 = jnp.float32
BF16 = jnp.bfloat16
HIGHEST = lax.Precision.HIGHEST
MESH = pl.DeviceIdType.MESH
VMEM_BYTES = 60 << 20

NT = (((1,), (1,)), ((), ()))
TN = (((0,), (0,)), ((), ()))
NN = (((1,), (0,)), ((), ()))

NEAR, ACROSS, RIGHT0, RIGHT1, FAR0, FAR1, LEFT0, LEFT1 = range(8)


def dot(a, b, dims, precision=None):
    return lax.dot_general(a, b, dims, precision=precision, preferred_element_type=F32)


def split(value, axis):
    high = value.astype(BF16)
    rest = value - high.astype(F32)
    middle = rest.astype(BF16)
    low = (rest - middle.astype(F32)).astype(BF16)
    return jnp.concatenate([high, middle, low], axis=axis)


def exact_tn(value, exact):
    product = dot(split(value.T, 0), exact, NN)
    count = product.shape[0] // 3
    return product[:count] + product[count : 2 * count] + product[2 * count :]


def stack_heads(rows):
    heads = rows.shape[1] // HEAD
    return jnp.concatenate([rows[:, h * HEAD : (h + 1) * HEAD] for h in range(heads)], axis=0)


def unstack_heads(stacked, count):
    heads = stacked.shape[0] // count
    return jnp.concatenate([stacked[h * count : (h + 1) * count] for h in range(heads)], axis=1)


def kernel(
    stages,
    members,
    shard,
    weight_hbm,
    down,
    up_hbm,
    query_hbm,
    key_hbm,
    value_hbm,
    segments,
    dq_ref,
    dk_ref,
    dv_ref,
    down_map_ref,
    up_map_ref,
    x_ref,
    weight,
    up,
    query,
    key,
    value,
    doc,
    context,
    lse,
    gradient,
    rank,
    acc,
    rank_acc,
    dq,
    dk,
    dv,
    rank_context,
    rank_sum,
    rank_parts,
    shard_send,
    shard_recv,
    parked_send,
    parked_recv,
    up_send,
    up_recv,
    rank_send,
    rank_recv,
    weight_sem,
    up_sem,
    dq_sem,
):
    pipe = lax.axis_index("pipe")
    member = lax.axis_index("fsdp")
    ring = members // 2
    plane, x = member // ring, member % ring
    rows, depth = shard.shape
    tokens, width = query_hbm.shape
    heads = width // HEAD
    ranks = down.shape[0]
    lanes = heads * rows
    wide = depth // CHUNKS
    local = depth // members
    before = (pipe + stages - 1) % stages
    behind = (pipe + 1) % stages
    flipped = (member + ring) % members
    to_left = plane * ring + (x + ring - 1) % ring
    to_right = plane * ring + (x + 1) % ring

    def device(p, f):
        return {"pipe": p, "fsdp": f}

    barrier = pltpu.get_barrier_semaphore()
    partners = [
        (before, member),
        (before, flipped),
        (behind, member),
        (behind, flipped),
        (stages - 1 - pipe, member),
    ]
    partners += [(pipe, (member + i) % members) for i in range(1, members)]
    for p, f in partners:
        pl.semaphore_signal(barrier, inc=1, device_id=device(p, f), device_id_type=MESH)

    def weight_copy(i):
        part = pl.ds(pl.multiple_of(i * local, local), local)
        return pltpu.make_async_copy(
            weight_hbm.at[:, part], weight.at[:, part], weight_sem.at[i]
        )

    @pl.loop(0, members)
    def _(i):
        weight_copy(i).start()

    own_up = pltpu.make_async_copy(up_hbm, up.at[member], up_sem)
    own_up.start()

    routes = {
        NEAR: (shard, before, member),
        ACROSS: (shard, before, flipped),
        RIGHT0: (x_ref.at[NEAR], pipe, to_left),
        LEFT0: (x_ref.at[NEAR], pipe, to_right),
        RIGHT1: (x_ref.at[ACROSS], pipe, to_left),
        LEFT1: (x_ref.at[ACROSS], pipe, to_right),
        FAR0: (x_ref.at[LEFT0], pipe, to_right),
        FAR1: (x_ref.at[LEFT1], pipe, to_right),
    }
    mirrored = {
        FAR0: (x_ref.at[RIGHT0], pipe, to_left),
        FAR1: (x_ref.at[RIGHT1], pipe, to_left),
    }

    def columns(c):
        return pl.ds(pl.multiple_of(c * wide, wide), wide)

    def hop(slot, c, table=routes):
        source, p, f = table[slot]
        return pltpu.make_async_remote_copy(
            src_ref=source.at[:, columns(c)],
            dst_ref=x_ref.at[slot, :, columns(c)],
            send_sem=shard_send.at[slot, c],
            recv_sem=shard_recv.at[slot, c],
            device_id=device(p, f),
            device_id_type=MESH,
        )

    def up_copy(i):
        return pltpu.make_async_remote_copy(
            src_ref=up_hbm,
            dst_ref=up.at[member],
            send_sem=up_send.at[i - 1],
            recv_sem=up_recv.at[i - 1],
            device_id=device(pipe, (member + i) % members),
            device_id_type=MESH,
        )

    parked = [
        pltpu.make_async_remote_copy(
            src_ref=source,
            dst_ref=target,
            send_sem=parked_send.at[i],
            recv_sem=parked_recv.at[i],
            device_id=device(stages - 1 - pipe, member),
            device_id_type=MESH,
        )
        for i, (source, target) in enumerate(
            [(key_hbm, key), (value_hbm, value), (query_hbm, query)]
        )
    ]

    def rank_copy(i):
        peer = flipped if i == 0 else plane * ring + (x + i) % ring
        return pltpu.make_async_remote_copy(
            src_ref=rank_sum.at[1 if i == 0 else 0],
            dst_ref=rank_parts.at[i],
            send_sem=rank_send.at[i],
            recv_sem=rank_recv.at[i],
            device_id=device(pipe, peer),
            device_id_type=MESH,
        )

    pl.semaphore_wait(barrier, len(partners))

    even = pipe % 2 == 0

    @pl.loop(0, CHUNKS)
    def _(c):
        hop(NEAR, c).start()

    def send_across():
        @pl.loop(0, CHUNKS)
        def _(c):
            hop(ACROSS, c).start()

    pl.when(even)(send_across)
    for i in range(1, members):
        up_copy(i).start()

    ids = jnp.broadcast_to(segments[...].astype(F32), (8, tokens))
    doc[...] = ids.T

    @pl.loop(0, CHUNKS)
    def _(c):
        hop(NEAR, c).wait_recv()
        hop(RIGHT0, c).start()
        hop(LEFT0, c).start()

    def relay_across():
        @pl.loop(0, CHUNKS)
        def _(c):
            hop(ACROSS, c).wait_recv()
            hop(RIGHT1, c).start()
            hop(LEFT1, c).start()

    def relay_far(far, left, right, c):
        hop(left, c).wait_recv()
        hop(far, c).start()
        hop(right, c + 1).wait_recv()
        hop(far, c + 1, mirrored).start()

    def send_parked():
        for copy in parked:
            copy.start()

    def relay_far_all(far, left, right):
        @pl.loop(0, CHUNKS, step=2)
        def _(c):
            relay_far(far, left, right, c)

    odd = pipe % 2 == 1

    @pl.when(even)
    def _():
        relay_far_all(FAR0, LEFT0, RIGHT0)
        send_parked()

    @pl.when(odd)
    def _():
        send_across()
        send_parked()
        relay_across()
        relay_far_all(FAR0, LEFT0, RIGHT0)

    def block_of(slot):
        side = (plane + slot) % 2
        return side * ring + (x + slot // 2) % ring

    def project_chunk(slots, c):
        used = pl.ds(0, len(slots) * rows)
        rows_in = jnp.concatenate([x_ref[slot, :, columns(c)] for slot in slots], axis=0)
        up_rows = [up[members // CHUNKS * c + i] for i in range(members // CHUNKS)]
        product = dot(weight[:, columns(c)], rows_in, NT)
        ranked = dot(jnp.concatenate(up_rows, axis=1), rows_in, NT)
        acc[:, used] = acc[:, used] + product
        rank_acc[:, used] = rank_acc[:, used] + ranked

    def project_start():
        acc[...] = jnp.zeros_like(acc)
        rank_acc[...] = jnp.zeros_like(rank_acc)

    def project_end(slots):
        used = pl.ds(0, len(slots) * rows)
        thrice = jnp.concatenate([down[...]] * 3, axis=0)
        projected = dot(thrice, split(rank_acc[:, used], 0), TN)
        total = (acc[:, used] + LORA_SCALE * projected).T.astype(BF16)
        ranked = rank_acc[:, used].T
        for i, slot in enumerate(slots):
            gradient[slot] = total[i * rows : (i + 1) * rows]
            rank[slot] = ranked[i * rows : (i + 1) * rows]

    own_up.wait()
    for i in range(1, members):
        up_copy(i).wait_recv()

    @pl.loop(0, members)
    def _(i):
        weight_copy(i).wait()

    own = (NEAR, RIGHT0, FAR0, LEFT0)
    project_start()

    @pl.loop(0, CHUNKS, step=2)
    def _(c):
        hop(RIGHT0, c).wait_recv()
        hop(FAR0, c).wait_recv()
        project_chunk(own, c)
        hop(LEFT0, c + 1).wait_recv()
        hop(FAR0, c + 1).wait_recv()
        project_chunk(own, c + 1)

    project_end(own)

    @pl.when(even)
    def _():
        relay_across()

    @pl.when(odd)
    def _():
        relay_far_all(FAR1, LEFT1, RIGHT1)

    def token_rows(block):
        return pl.ds(pl.multiple_of(block * rows, 32), rows)

    def key_window(block):
        begin = (block // (KEYS // rows)) * (block * rows + rows - KEYS)
        return pl.multiple_of(begin, 32)

    def allowed_keys(block, begin, reach=KEYS):
        lane = lax.broadcasted_iota(jnp.int32, (rows, lanes), 1) % rows
        spread = (lax.broadcasted_iota(jnp.int32, (rows, lanes), 0) == lane).astype(F32)
        own = dot(doc[token_rows(block), :], spread, TN)[0:1]
        other = doc[pl.ds(begin, reach), 0:1]
        place = block * rows + lane[0:1]
        position = begin + lax.broadcasted_iota(jnp.int32, (reach, lanes), 0)
        return (position <= place) & (other == own)

    def scores_of(block, begin, reach=KEYS):
        queries = stack_heads(query[token_rows(block), :])
        scores = dot(key[pl.ds(begin, reach), :], queries, NT) * (LOG2E / math.sqrt(HEAD))
        return queries, scores

    for copy in parked:
        copy.wait_recv()

    def forward(reach, block):
        begin = key_window(block)
        _, scores = scores_of(block, begin, reach)
        scores = jnp.where(allowed_keys(block, begin, reach), scores, NEG)
        top = jnp.max(scores, axis=0, keepdims=True)
        expanded = jnp.exp2(scores - top)
        total = jnp.sum(expanded, axis=0, keepdims=True)
        probs = (expanded / total).astype(BF16)
        mixed = dot(value[pl.ds(begin, reach), :], probs, TN)
        mixed = unstack_heads(mixed.T.astype(BF16), rows)
        context[token_rows(block), :] = mixed
        lse[block] = top + jnp.log2(total)
        rank_context[token_rows(block), :] = dot(mixed, down[...], NT)

    done = 0
    for reach in (KEYS // 2, 3 * KEYS // 4, KEYS):
        until = members if reach == KEYS else reach // rows
        pl.loop(done, until)(functools.partial(forward, reach))
        done = until

    rank_sum[0] = rank_context[...].T
    for i in range(1, ring):
        rank_copy(i).start()

    dk[...] = jnp.zeros_like(dk)
    dv[...] = jnp.zeros_like(dv)
    down_map_ref[...] = jnp.zeros_like(down_map_ref)
    up_map_ref[...] = jnp.zeros_like(up_map_ref)

    def dq_copy(slot):
        block = block_of(slot)
        return pltpu.make_async_copy(
            dq.at[token_rows(block), :], dq_ref.at[token_rows(block), :], dq_sem.at[slot]
        )

    def backward(slot):
        block = block_of(slot)
        begin = key_window(block)
        window = pl.ds(begin, KEYS)
        queries, scores = scores_of(block, begin)
        arriving = stack_heads(gradient[slot])
        mixed = context[token_rows(block), :]
        products = arriving.astype(F32) * stack_heads(mixed).astype(F32)
        delta = dot(jnp.ones((16, 3 * HEAD), BF16), split(products, 1), NT)[0:1]
        shifted = jnp.where(allowed_keys(block, begin), scores - lse[block], NEG)
        probs = jnp.exp2(shifted)
        grad_probs = dot(value[window, :], arriving, NT)
        grad_scores = (probs * (grad_probs - delta)).astype(BF16)
        dv[window, :] += dot(probs.astype(BF16), arriving, NN)
        dk[window, :] += dot(grad_scores, queries, NN)
        grad_query = dot(key[window, :], grad_scores, TN) * (1.0 / math.sqrt(HEAD))
        dq[token_rows(block), :] = unstack_heads(grad_query.T.astype(BF16), rows)
        down_map_ref[...] += exact_tn(rank[slot], mixed)
        dq_copy(slot).start()

    def up_map(slot):
        part = x_ref[slot, :, pl.ds(pl.multiple_of(member * local, local), local)]
        ranked = rank_context[token_rows(block_of(slot)), :]
        up_map_ref[...] += exact_tn(ranked, part)

    @pl.when(even)
    def _():
        relay_far_all(FAR1, LEFT1, RIGHT1)

    pl.loop(NEAR, members, step=2)(backward)
    project_start()

    @pl.loop(0, CHUNKS, step=2)
    def _(c):
        hop(RIGHT1, c).wait_recv()
        project_chunk((ACROSS, RIGHT1), c)
        project_chunk((ACROSS, RIGHT1), c + 1)

    project_end((ACROSS, RIGHT1))
    pl.loop(ACROSS, FAR1, step=2)(backward)
    for i in range(1, ring):
        rank_copy(i).wait_recv()
    rank_sum[1] = rank_sum[0] + rank_parts[1] + rank_parts[2] + rank_parts[3]
    rank_copy(0).start()
    project_start()

    @pl.loop(0, CHUNKS, step=2)
    def _(c):
        hop(FAR1, c).wait_recv()
        project_chunk((FAR1, LEFT1), c)
        hop(LEFT1, c + 1).wait_recv()
        hop(FAR1, c + 1).wait_recv()
        project_chunk((FAR1, LEFT1), c + 1)

    project_end((FAR1, LEFT1))
    pl.loop(FAR1, members, step=2)(backward)
    rank_copy(0).wait_recv()
    rank_context[...] = (rank_sum[1] + rank_parts[0]).T
    pl.loop(0, members)(up_map)

    dk_ref[...] = (dk[...] * (1.0 / math.sqrt(HEAD))).astype(BF16)
    dv_ref[...] = dv[...].astype(BF16)

    for slot in range(members):

        @pl.loop(0, CHUNKS)
        def _(c):
            hop(slot, c).wait_send()

        dq_copy(slot).wait()
    for copy in parked:
        copy.wait_send()
    for i in range(1, members):
        up_copy(i).wait_send()
    for i in range(ring):
        rank_copy(i).wait_send()


def finish_kernel(scale, dq_in, dk_in, dv_in, down_map_in, up_map_in, dq, dk, dv, down_map, up_map):
    dq[...] = dq_in[...]

    @pl.when(pl.program_id(0) == 0)
    def _():
        dk[...] = dk_in[...]
        dv[...] = dv_in[...]
        down_map[...] = down_map_in[...] * scale
        up_map[...] = up_map_in[...] * scale


def per_device(
    handoff_gradient,
    output_weight,
    adapter_down,
    adapter_up,
    stored_queries,
    stored_keys,
    stored_values,
    segments,
):
    stages = lax.axis_size("pipe")
    members = lax.axis_size("fsdp")
    rows, depth = handoff_gradient.shape[1:]
    tokens, width = stored_queries.shape[1:]
    ranks = adapter_down.shape[1]
    local = adapter_up.shape[2]
    lanes = width // HEAD * rows
    anywhere = pl.BlockSpec(memory_space=pl.ANY)
    on_chip = pl.BlockSpec(memory_space=pltpu.VMEM)
    dma = pltpu.SemaphoreType.DMA
    outputs = pl.pallas_call(
        functools.partial(kernel, stages, members),
        in_specs=[anywhere, anywhere, on_chip, anywhere, anywhere, anywhere, anywhere, on_chip],
        out_specs=[anywhere, on_chip, on_chip, on_chip, on_chip],
        out_shape=[
            jax.ShapeDtypeStruct((tokens, width), BF16),
            jax.ShapeDtypeStruct((tokens, HEAD), BF16),
            jax.ShapeDtypeStruct((tokens, HEAD), BF16),
            jax.ShapeDtypeStruct((ranks, width), F32),
            jax.ShapeDtypeStruct((ranks, local), F32),
        ],
        scratch_shapes=[
            pltpu.VMEM((members, rows, depth), BF16),
            pltpu.VMEM((width, depth), BF16),
            pltpu.VMEM((members, ranks, local), BF16),
            pltpu.VMEM((tokens, width), BF16),
            pltpu.VMEM((tokens, HEAD), BF16),
            pltpu.VMEM((tokens, HEAD), BF16),
            pltpu.VMEM((tokens, 8), F32),
            pltpu.VMEM((tokens, width), BF16),
            pltpu.VMEM((members, 1, lanes), F32),
            pltpu.VMEM((members, rows, width), BF16),
            pltpu.VMEM((members, rows, ranks), F32),
            pltpu.VMEM((width, 4 * rows), F32),
            pltpu.VMEM((ranks, 4 * rows), F32),
            pltpu.VMEM((tokens, width), BF16),
            pltpu.VMEM((tokens, HEAD), F32),
            pltpu.VMEM((tokens, HEAD), F32),
            pltpu.VMEM((tokens, ranks), F32),
            pltpu.VMEM((2, ranks, tokens), F32),
            pltpu.VMEM((4, ranks, tokens), F32),
            dma((members, CHUNKS)),
            dma((members, CHUNKS)),
            dma((3,)),
            dma((3,)),
            dma((members - 1,)),
            dma((members - 1,)),
            dma((4,)),
            dma((4,)),
            dma((members,)),
            dma,
            dma((members,)),
        ],
        compiler_params=pltpu.CompilerParams(
            collective_id=0, has_side_effects=True, vmem_limit_bytes=VMEM_BYTES
        ),
        name="relay",
    )(
        handoff_gradient[0],
        output_weight[0],
        adapter_down[0],
        adapter_up[0],
        stored_queries[0],
        stored_keys[0],
        stored_values[0],
        segments,
    )
    pieces = 4
    specs = [pl.BlockSpec((tokens // pieces, width), lambda i: (i, 0))]
    specs += [pl.BlockSpec(output.shape, lambda i: (0, 0)) for output in outputs[1:]]
    outputs = pl.pallas_call(
        functools.partial(finish_kernel, LORA_SCALE / math.sqrt(tokens)),
        grid=(pieces,),
        in_specs=specs,
        out_specs=specs,
        out_shape=[jax.ShapeDtypeStruct(output.shape, output.dtype) for output in outputs],
        compiler_params=pltpu.CompilerParams(vmem_limit_bytes=VMEM_BYTES),
        name="finish",
    )(*outputs)
    return tuple(output[None] for output in outputs)


def solution(mesh):
    split = P("pipe", None, "fsdp")
    rows = P("pipe", "fsdp", None)
    return jax.shard_map(
        per_device,
        mesh=mesh,
        in_specs=(rows, rows, split, split, split, split, split, P("pipe", None)),
        out_specs=(split,) * 5,
        check_vma=False,
    )
```

```python
import functools
import math

import jax
import jax.numpy as jnp
from jax import lax
from jax.experimental import pallas as pl
from jax.experimental.pallas import tpu as pltpu
from jax.sharding import PartitionSpec as P

HEAD = 128
KEYS = 512
CHUNKS = 4
LORA_SCALE = 2.0
NEG = -1e30
LOG2E = math.log2(math.e)
F32 = jnp.float32
BF16 = jnp.bfloat16
HIGHEST = lax.Precision.HIGHEST
MESH = pl.DeviceIdType.MESH
VMEM_BYTES = 60 << 20

NT = (((1,), (1,)), ((), ()))
TN = (((0,), (0,)), ((), ()))
NN = (((1,), (0,)), ((), ()))

NEAR, ACROSS, RIGHT0, RIGHT1, FAR0, FAR1, LEFT0, LEFT1 = range(8)


def dot(a, b, dims, precision=None):
    return lax.dot_general(a, b, dims, precision=precision, preferred_element_type=F32)


def split(value, axis):
    high = value.astype(BF16)
    rest = value - high.astype(F32)
    middle = rest.astype(BF16)
    low = (rest - middle.astype(F32)).astype(BF16)
    return jnp.concatenate([high, middle, low], axis=axis)


def exact_tn(value, exact):
    product = dot(split(value.T, 0), exact, NN)
    count = product.shape[0] // 3
    return product[:count] + product[count : 2 * count] + product[2 * count :]


def stack_heads(rows):
    heads = rows.shape[1] // HEAD
    return jnp.concatenate([rows[:, h * HEAD : (h + 1) * HEAD] for h in range(heads)], axis=0)


def unstack_heads(stacked, count):
    heads = stacked.shape[0] // count
    return jnp.concatenate([stacked[h * count : (h + 1) * count] for h in range(heads)], axis=1)


def kernel(
    stages,
    members,
    shard,
    weight_hbm,
    down,
    up_hbm,
    query_hbm,
    key_hbm,
    value_hbm,
    segments,
    dq_ref,
    dk_ref,
    dv_ref,
    down_map_ref,
    up_map_ref,
    x_ref,
    weight,
    up,
    query,
    key,
    value,
    doc,
    context,
    lse,
    gradient,
    rank,
    acc,
    rank_acc,
    dq,
    dk,
    dv,
    rank_context,
    rank_sum,
    rank_parts,
    shard_send,
    shard_recv,
    parked_send,
    parked_recv,
    query_send,
    query_recv,
    up_send,
    up_recv,
    rank_send,
    rank_recv,
    weight_sem,
    up_sem,
    dq_sem,
):
    pipe = lax.axis_index("pipe")
    member = lax.axis_index("fsdp")
    ring = members // 2
    plane, x = member // ring, member % ring
    rows, depth = shard.shape
    tokens, width = query_hbm.shape
    heads = width // HEAD
    ranks = down.shape[0]
    lanes = heads * rows
    wide = depth // CHUNKS
    local = depth // members
    before = (pipe + stages - 1) % stages
    behind = (pipe + 1) % stages
    flipped = (member + ring) % members
    to_left = plane * ring + (x + ring - 1) % ring
    to_right = plane * ring + (x + 1) % ring

    def device(p, f):
        return {"pipe": p, "fsdp": f}

    barrier = pltpu.get_barrier_semaphore()
    partners = [
        (before, member),
        (before, flipped),
        (behind, member),
        (behind, flipped),
        (stages - 1 - pipe, member),
    ]
    partners += [(pipe, (member + i) % members) for i in range(1, members)]
    for p, f in partners:
        pl.semaphore_signal(barrier, inc=1, device_id=device(p, f), device_id_type=MESH)

    def weight_copy(i):
        part = pl.ds(pl.multiple_of(i * local, local), local)
        return pltpu.make_async_copy(
            weight_hbm.at[:, part], weight.at[:, part], weight_sem.at[i]
        )

    @pl.loop(0, members)
    def _(i):
        weight_copy(i).start()

    own_up = pltpu.make_async_copy(up_hbm, up.at[member], up_sem)
    own_up.start()

    routes = {
        NEAR: (shard, before, member),
        ACROSS: (shard, before, flipped),
        RIGHT0: (x_ref.at[NEAR], pipe, to_left),
        LEFT0: (x_ref.at[NEAR], pipe, to_right),
        RIGHT1: (x_ref.at[ACROSS], pipe, to_left),
        LEFT1: (x_ref.at[ACROSS], pipe, to_right),
        FAR0: (x_ref.at[LEFT0], pipe, to_right),
        FAR1: (x_ref.at[LEFT1], pipe, to_right),
    }
    mirrored = {
        FAR0: (x_ref.at[RIGHT0], pipe, to_left),
        FAR1: (x_ref.at[RIGHT1], pipe, to_left),
    }

    def columns(c):
        return pl.ds(pl.multiple_of(c * wide, wide), wide)

    def hop(slot, c, table=routes):
        source, p, f = table[slot]
        return pltpu.make_async_remote_copy(
            src_ref=source.at[:, columns(c)],
            dst_ref=x_ref.at[slot, :, columns(c)],
            send_sem=shard_send.at[slot, c],
            recv_sem=shard_recv.at[slot, c],
            device_id=device(p, f),
            device_id_type=MESH,
        )

    def up_copy(i):
        return pltpu.make_async_remote_copy(
            src_ref=up_hbm,
            dst_ref=up.at[member],
            send_sem=up_send.at[i - 1],
            recv_sem=up_recv.at[i - 1],
            device_id=device(pipe, (member + i) % members),
            device_id_type=MESH,
        )

    parked = [
        pltpu.make_async_remote_copy(
            src_ref=source,
            dst_ref=target,
            send_sem=parked_send.at[i],
            recv_sem=parked_recv.at[i],
            device_id=device(stages - 1 - pipe, member),
            device_id_type=MESH,
        )
        for i, (source, target) in enumerate(
            [(key_hbm, key), (value_hbm, value)]
        )
    ]

    def query_copy(block):
        part = pl.ds(pl.multiple_of(block * rows, 32), rows)
        return pltpu.make_async_remote_copy(
            src_ref=query_hbm.at[part, :],
            dst_ref=query.at[part, :],
            send_sem=query_send.at[block],
            recv_sem=query_recv.at[block],
            device_id=device(stages - 1 - pipe, member),
            device_id_type=MESH,
        )

    def rank_copy(i):
        peer = flipped if i == 0 else plane * ring + (x + i) % ring
        return pltpu.make_async_remote_copy(
            src_ref=rank_sum.at[1 if i == 0 else 0],
            dst_ref=rank_parts.at[i],
            send_sem=rank_send.at[i],
            recv_sem=rank_recv.at[i],
            device_id=device(pipe, peer),
            device_id_type=MESH,
        )

    pl.semaphore_wait(barrier, len(partners))

    even = pipe % 2 == 0

    @pl.loop(0, CHUNKS)
    def _(c):
        hop(NEAR, c).start()

    def send_across():
        @pl.loop(0, CHUNKS)
        def _(c):
            hop(ACROSS, c).start()

    pl.when(even)(send_across)
    for i in range(1, members):
        up_copy(i).start()

    ids = jnp.broadcast_to(segments[...].astype(F32), (8, tokens))
    doc[...] = ids.T

    @pl.loop(0, CHUNKS)
    def _(c):
        hop(NEAR, c).wait_recv()
        hop(RIGHT0, c).start()
        hop(LEFT0, c).start()

    def relay_across():
        @pl.loop(0, CHUNKS)
        def _(c):
            hop(ACROSS, c).wait_recv()
            hop(RIGHT1, c).start()
            hop(LEFT1, c).start()

    def relay_far(far, left, right, c):
        hop(left, c).wait_recv()
        hop(far, c).start()
        hop(right, c + 1).wait_recv()
        hop(far, c + 1, mirrored).start()

    def send_parked():
        for copy in parked:
            copy.start()

        @pl.loop(0, members)
        def _(block):
            query_copy(block).start()

    def relay_far_all(far, left, right):
        @pl.loop(0, CHUNKS, step=2)
        def _(c):
            relay_far(far, left, right, c)

    odd = pipe % 2 == 1

    @pl.when(even)
    def _():
        relay_far_all(FAR0, LEFT0, RIGHT0)
        send_parked()

    @pl.when(odd)
    def _():
        send_across()
        send_parked()
        relay_across()
        relay_far_all(FAR0, LEFT0, RIGHT0)

    def block_of(slot):
        side = (plane + slot) % 2
        return side * ring + (x + slot // 2) % ring

    def project_chunk(slots, c):
        used = pl.ds(0, len(slots) * rows)
        rows_in = jnp.concatenate([x_ref[slot, :, columns(c)] for slot in slots], axis=0)
        up_rows = [up[members // CHUNKS * c + i] for i in range(members // CHUNKS)]
        product = dot(weight[:, columns(c)], rows_in, NT)
        ranked = dot(jnp.concatenate(up_rows, axis=1), rows_in, NT)
        acc[:, used] = acc[:, used] + product
        rank_acc[:, used] = rank_acc[:, used] + ranked

    def project_start():
        acc[...] = jnp.zeros_like(acc)
        rank_acc[...] = jnp.zeros_like(rank_acc)

    def project_end(slots):
        used = pl.ds(0, len(slots) * rows)
        thrice = jnp.concatenate([down[...]] * 3, axis=0)
        projected = dot(thrice, split(rank_acc[:, used], 0), TN)
        total = (acc[:, used] + LORA_SCALE * projected).T.astype(BF16)
        ranked = rank_acc[:, used].T
        for i, slot in enumerate(slots):
            gradient[slot] = total[i * rows : (i + 1) * rows]
            rank[slot] = ranked[i * rows : (i + 1) * rows]

    own_up.wait()
    for i in range(1, members):
        up_copy(i).wait_recv()

    @pl.loop(0, members)
    def _(i):
        weight_copy(i).wait()

    own = (NEAR, RIGHT0, FAR0, LEFT0)
    project_start()

    @pl.loop(0, CHUNKS, step=2)
    def _(c):
        hop(RIGHT0, c).wait_recv()
        hop(FAR0, c).wait_recv()
        project_chunk(own, c)
        hop(LEFT0, c + 1).wait_recv()
        hop(FAR0, c + 1).wait_recv()
        project_chunk(own, c + 1)

    project_end(own)

    @pl.when(odd)
    def _():
        relay_far_all(FAR1, LEFT1, RIGHT1)

    def token_rows(block):
        return pl.ds(pl.multiple_of(block * rows, 32), rows)

    def key_window(block):
        begin = (block // (KEYS // rows)) * (block * rows + rows - KEYS)
        return pl.multiple_of(begin, 32)

    def allowed_keys(block, begin, reach=KEYS):
        lane = lax.broadcasted_iota(jnp.int32, (rows, lanes), 1) % rows
        spread = (lax.broadcasted_iota(jnp.int32, (rows, lanes), 0) == lane).astype(F32)
        own = dot(doc[token_rows(block), :], spread, TN)[0:1]
        other = doc[pl.ds(begin, reach), 0:1]
        place = block * rows + lane[0:1]
        position = begin + lax.broadcasted_iota(jnp.int32, (reach, lanes), 0)
        return (position <= place) & (other == own)

    def scores_of(block, begin, reach=KEYS):
        queries = stack_heads(query[token_rows(block), :])
        scores = dot(key[pl.ds(begin, reach), :], queries, NT) * (LOG2E / math.sqrt(HEAD))
        return queries, scores

    for copy in parked:
        copy.wait_recv()

    def forward(reach, block):
        query_copy(block).wait_recv()
        begin = key_window(block)
        _, scores = scores_of(block, begin, reach)
        scores = jnp.where(allowed_keys(block, begin, reach), scores, NEG)
        top = jnp.max(scores, axis=0, keepdims=True)
        expanded = jnp.exp2(scores - top)
        total = jnp.sum(expanded, axis=0, keepdims=True)
        probs = (expanded / total).astype(BF16)
        mixed = dot(value[pl.ds(begin, reach), :], probs, TN)
        mixed = unstack_heads(mixed.T.astype(BF16), rows)
        context[token_rows(block), :] = mixed
        lse[block] = top + jnp.log2(total)
        rank_context[token_rows(block), :] = dot(mixed, down[...], NT)

    done = 0
    for reach in (KEYS // 2, 3 * KEYS // 4, KEYS):
        until = members if reach == KEYS else reach // rows
        pl.loop(done, until)(functools.partial(forward, reach))
        done = until

    rank_sum[0] = rank_context[...].T
    for i in range(1, ring):
        rank_copy(i).start()

    dk[...] = jnp.zeros_like(dk)
    dv[...] = jnp.zeros_like(dv)
    down_map_ref[...] = jnp.zeros_like(down_map_ref)
    up_map_ref[...] = jnp.zeros_like(up_map_ref)

    def dq_copy(slot):
        block = block_of(slot)
        return pltpu.make_async_copy(
            dq.at[token_rows(block), :], dq_ref.at[token_rows(block), :], dq_sem.at[slot]
        )

    def backward(slot):
        block = block_of(slot)
        begin = key_window(block)
        window = pl.ds(begin, KEYS)
        queries, scores = scores_of(block, begin)
        arriving = stack_heads(gradient[slot])
        mixed = context[token_rows(block), :]
        products = arriving.astype(F32) * stack_heads(mixed).astype(F32)
        delta = dot(jnp.ones((16, 3 * HEAD), BF16), split(products, 1), NT)[0:1]
        shifted = jnp.where(allowed_keys(block, begin), scores - lse[block], NEG)
        probs = jnp.exp2(shifted)
        grad_probs = dot(value[window, :], arriving, NT)
        grad_scores = (probs * (grad_probs - delta)).astype(BF16)
        dv[window, :] += dot(probs.astype(BF16), arriving, NN)
        dk[window, :] += dot(grad_scores, queries, NN)
        grad_query = dot(key[window, :], grad_scores, TN) * (1.0 / math.sqrt(HEAD))
        dq[token_rows(block), :] = unstack_heads(grad_query.T.astype(BF16), rows)
        down_map_ref[...] += exact_tn(rank[slot], mixed)
        dq_copy(slot).start()

    def up_map(slot):
        part = x_ref[slot, :, pl.ds(pl.multiple_of(member * local, local), local)]
        ranked = rank_context[token_rows(block_of(slot)), :]
        up_map_ref[...] += exact_tn(ranked, part)

    pl.when(even)(relay_across)
    pl.loop(NEAR, FAR0, step=2)(backward)

    @pl.when(even)
    def _():
        relay_far_all(FAR1, LEFT1, RIGHT1)

    pl.loop(FAR0, members, step=2)(backward)
    project_start()

    @pl.loop(0, CHUNKS, step=2)
    def _(c):
        hop(RIGHT1, c).wait_recv()
        project_chunk((ACROSS, RIGHT1), c)
        project_chunk((ACROSS, RIGHT1), c + 1)

    project_end((ACROSS, RIGHT1))
    pl.loop(ACROSS, FAR1, step=2)(backward)
    for i in range(1, ring):
        rank_copy(i).wait_recv()
    rank_sum[1] = rank_sum[0] + rank_parts[1] + rank_parts[2] + rank_parts[3]
    rank_copy(0).start()
    project_start()

    @pl.loop(0, CHUNKS, step=2)
    def _(c):
        hop(FAR1, c).wait_recv()
        project_chunk((FAR1, LEFT1), c)
        hop(LEFT1, c + 1).wait_recv()
        hop(FAR1, c + 1).wait_recv()
        project_chunk((FAR1, LEFT1), c + 1)

    project_end((FAR1, LEFT1))
    pl.loop(FAR1, members, step=2)(backward)
    rank_copy(0).wait_recv()
    rank_context[...] = (rank_sum[1] + rank_parts[0]).T
    pl.loop(0, members)(up_map)

    dk_ref[...] = (dk[...] * (1.0 / math.sqrt(HEAD))).astype(BF16)
    dv_ref[...] = dv[...].astype(BF16)

    for slot in range(members):

        @pl.loop(0, CHUNKS)
        def _(c):
            hop(slot, c).wait_send()

        dq_copy(slot).wait()
        query_copy(slot).wait_send()
    for copy in parked:
        copy.wait_send()
    for i in range(1, members):
        up_copy(i).wait_send()
    for i in range(ring):
        rank_copy(i).wait_send()


def finish_kernel(scale, dq_in, dk_in, dv_in, down_map_in, up_map_in, dq, dk, dv, down_map, up_map):
    dq[...] = dq_in[...]

    @pl.when(pl.program_id(0) == 0)
    def _():
        dk[...] = dk_in[...]
        dv[...] = dv_in[...]
        down_map[...] = down_map_in[...] * scale
        up_map[...] = up_map_in[...] * scale


def per_device(
    handoff_gradient,
    output_weight,
    adapter_down,
    adapter_up,
    stored_queries,
    stored_keys,
    stored_values,
    segments,
):
    stages = lax.axis_size("pipe")
    members = lax.axis_size("fsdp")
    rows, depth = handoff_gradient.shape[1:]
    tokens, width = stored_queries.shape[1:]
    ranks = adapter_down.shape[1]
    local = adapter_up.shape[2]
    lanes = width // HEAD * rows
    anywhere = pl.BlockSpec(memory_space=pl.ANY)
    on_chip = pl.BlockSpec(memory_space=pltpu.VMEM)
    dma = pltpu.SemaphoreType.DMA
    outputs = pl.pallas_call(
        functools.partial(kernel, stages, members),
        in_specs=[anywhere, anywhere, on_chip, anywhere, anywhere, anywhere, anywhere, on_chip],
        out_specs=[anywhere, on_chip, on_chip, on_chip, on_chip],
        out_shape=[
            jax.ShapeDtypeStruct((tokens, width), BF16),
            jax.ShapeDtypeStruct((tokens, HEAD), BF16),
            jax.ShapeDtypeStruct((tokens, HEAD), BF16),
            jax.ShapeDtypeStruct((ranks, width), F32),
            jax.ShapeDtypeStruct((ranks, local), F32),
        ],
        scratch_shapes=[
            pltpu.VMEM((members, rows, depth), BF16),
            pltpu.VMEM((width, depth), BF16),
            pltpu.VMEM((members, ranks, local), BF16),
            pltpu.VMEM((tokens, width), BF16),
            pltpu.VMEM((tokens, HEAD), BF16),
            pltpu.VMEM((tokens, HEAD), BF16),
            pltpu.VMEM((tokens, 8), F32),
            pltpu.VMEM((tokens, width), BF16),
            pltpu.VMEM((members, 1, lanes), F32),
            pltpu.VMEM((members, rows, width), BF16),
            pltpu.VMEM((members, rows, ranks), F32),
            pltpu.VMEM((width, 4 * rows), F32),
            pltpu.VMEM((ranks, 4 * rows), F32),
            pltpu.VMEM((tokens, width), BF16),
            pltpu.VMEM((tokens, HEAD), F32),
            pltpu.VMEM((tokens, HEAD), F32),
            pltpu.VMEM((tokens, ranks), F32),
            pltpu.VMEM((2, ranks, tokens), F32),
            pltpu.VMEM((4, ranks, tokens), F32),
            dma((members, CHUNKS)),
            dma((members, CHUNKS)),
            dma((2,)),
            dma((2,)),
            dma((members,)),
            dma((members,)),
            dma((members - 1,)),
            dma((members - 1,)),
            dma((4,)),
            dma((4,)),
            dma((members,)),
            dma,
            dma((members,)),
        ],
        compiler_params=pltpu.CompilerParams(
            collective_id=0, has_side_effects=True, vmem_limit_bytes=VMEM_BYTES
        ),
        name="relay",
    )(
        handoff_gradient[0],
        output_weight[0],
        adapter_down[0],
        adapter_up[0],
        stored_queries[0],
        stored_keys[0],
        stored_values[0],
        segments,
    )
    pieces = 4
    specs = [pl.BlockSpec((tokens // pieces, width), lambda i: (i, 0))]
    specs += [pl.BlockSpec(output.shape, lambda i: (0, 0)) for output in outputs[1:]]
    outputs = pl.pallas_call(
        functools.partial(finish_kernel, LORA_SCALE / math.sqrt(tokens)),
        grid=(pieces,),
        in_specs=specs,
        out_specs=specs,
        out_shape=[jax.ShapeDtypeStruct(output.shape, output.dtype) for output in outputs],
        compiler_params=pltpu.CompilerParams(vmem_limit_bytes=VMEM_BYTES),
        name="finish",
    )(*outputs)
    return tuple(output[None] for output in outputs)


def solution(mesh):
    split = P("pipe", None, "fsdp")
    rows = P("pipe", "fsdp", None)
    return jax.shard_map(
        per_device,
        mesh=mesh,
        in_specs=(rows, rows, split, split, split, split, split, P("pipe", None)),
        out_specs=(split,) * 5,
        check_vma=False,
    )
```
